128 devices in a mesh: gx: 16 (over x_hi, z, core), gy: 8 (over x_lo, y).
Axes of the slice: x: 4 (x_hi: 2, x_lo: 2; x = x_hi * 2 + x_lo), y: 4, z: 4, core: 2. Of those that a mesh axis runs over, the one named last changes fastest.
Arguments:
- populations: float32 [19, 256, 128, 128], P(None, 'gx', 'gy')
- panels: bfloat16 [64, 200, 128], P(None, None, ('gx', 'gy')), may hold values from -0.59765625 to 0.59765625
- modal_vel: bfloat16 [64, 2, 200], replicated, may hold values from -0.4375 to 0.4375
- marker_x: int32 [16, 8, 512], P('gx', 'gy'), may hold values from 0 to 15
- marker_y: int32 [16, 8, 512], P('gx', 'gy'), may hold values from 0 to 15
- marker_z: int32 [16, 8, 512], P('gx', 'gy'), may hold values from 0 to 127
- marker_riser: int32 [16, 8, 512], P('gx', 'gy'), may hold values from 0 to 63
Outputs:
- next_populations: float32 [19, 256, 128, 128], P(None, 'gx', 'gy')
- marker_force: float32 [16, 8, 3, 512], P('gx', 'gy')
- force_field: float32 [3, 256, 128, 128], P(None, 'gx', 'gy')
The draws below stay inside these ranges and needn't reach their ends.
All inputs are finite; a program needn't handle non-finite values.
Results may differ from the reference program's by a relative error of at most 0.0008.
Values may be sent and summed in bfloat16 or wider, within the bound.
No kernel may reach another device: no remote copies, remote signals or barrier semaphores. Data moves between devices by JAX's collectives and lax.ppermute only.
A program may use at most 128 MiB of HBM per device.

```python
import jax
import jax.numpy as jnp
from jax import lax

CX = 16
CY = 16
NZ = 128
MK = 512
RISERS = 64
MODES = 200
TILES_X = 16
TILES_Y = 8
NX = 256
NY = 128


VELOCITY = ((0, 0, 0), (1, 0, 0), (-1, 0, 0), (0, 1, 0), (0, -1, 0), (0, 0, 1), (0, 0, -1), (1, 1, 0), (-1, -1, 0), (1, -1, 0), (-1, 1, 0), (1, 0, 1), (-1, 0, -1), (1, 0, -1), (-1, 0, 1), (0, 1, 1), (0, -1, -1), (0, 1, -1), (0, -1, 1))


WEIGHT = (1.0 / 3.0,) + (1.0 / 18.0,) * 6 + (1.0 / 36.0,) * 12


def draw_populations(key, part):
    key_dens, key_vel, key_noise = jax.random.split(key, 3)
    cells = (NX, NY, NZ)
    density = jax.random.uniform(key_dens, cells, jnp.float32, 0.9, 1.1)
    velocity = jnp.clip(0.04 * jax.random.normal(key_vel, (3,) + cells, jnp.float32), -0.12, 0.12)
    noise = jnp.clip(0.04 * jax.random.normal(key_noise, (19,) + cells, jnp.float32), -0.12, 0.12)
    square = velocity[0] * velocity[0] + velocity[1] * velocity[1] + velocity[2] * velocity[2]
    layers = []
    for index in range(19):
        proj = VELOCITY[index][0] * velocity[0] + VELOCITY[index][1] * velocity[1] + VELOCITY[index][2] * velocity[2]
        equil = WEIGHT[index] * density * (1.0 + 3.0 * proj + 4.5 * proj * proj - 1.5 * square)
        layers.append(equil * (1.0 + noise[index]))
    return jnp.stack(layers).astype(jnp.float32)


def with_ends(array, stream_key, smallest, top_value):
    spot = [jax.random.randint(jax.random.fold_in(stream_key, axis), (), 0, length) for axis, length in enumerate(array.shape)]
    longest = array.shape.index(max(array.shape))
    next_to = spot[:longest] + [(spot[longest] + 1) % array.shape[longest]] + spot[longest + 1:]
    return array.at[tuple(spot)].set(smallest).at[tuple(next_to)].set(top_value)


def level_of(key, extent, pieces, smallest, high):
    def one(axis_at, parts):
        heights = jax.random.uniform(jax.random.fold_in(jax.random.fold_in(key, 6), axis_at), (parts,), jnp.float32, smallest / len(pieces), high / len(pieces))
        return jnp.repeat(jnp.exp(heights), extent[axis_at] // parts).reshape((-1,) + (1,) * (len(extent) - axis_at - 1))

    gain = one(*pieces[0])
    for cut in pieces[1:]:
        gain = gain * one(*cut)
    return gain


def bell_draw(own_key, extent, deviation, limit, cuts=(), dtype=jnp.bfloat16):
    array = deviation * jax.random.normal(own_key, extent, jnp.float32)
    if cuts:
        array = array * level_of(own_key, extent, cuts, -0.22, 0.18)
    return jnp.clip(array, -limit, limit).astype(dtype)


def setup_inputs(seed: int = 0) -> dict:
    key_list = jax.random.split(jax.random.key(seed), 8)
    populations = draw_populations(jax.random.fold_in(key_list[7], 71), 0)
    panels = bell_draw(key_list[1], (RISERS, MODES, NZ), 0.1, 0.59765625, ((2, 128),))
    modal_vel = bell_draw(key_list[2], (RISERS, 2, MODES), MODES ** -0.5, 0.4375)
    marker_x = with_ends(jax.random.randint(key_list[3], (TILES_X, TILES_Y, MK), 0, CX), jax.random.fold_in(key_list[3], 1), 0, CX - 1).astype(jnp.int32)
    marker_y = with_ends(jax.random.randint(key_list[4], (TILES_X, TILES_Y, MK), 0, CY), jax.random.fold_in(key_list[4], 1), 0, CY - 1).astype(jnp.int32)
    marker_z = with_ends(jax.random.randint(key_list[5], (TILES_X, TILES_Y, MK), 0, NZ), jax.random.fold_in(key_list[5], 1), 0, NZ - 1).astype(jnp.int32)
    marker_riser = with_ends(jax.random.randint(key_list[6], (TILES_X, TILES_Y, MK), 0, RISERS), jax.random.fold_in(key_list[6], 1), 0, RISERS - 1).astype(jnp.int32)
    return dict(populations=populations, panels=panels, modal_vel=modal_vel, marker_x=marker_x, marker_y=marker_y, marker_z=marker_z, marker_riser=marker_riser)


VELOCITY = ((0, 0, 0), (1, 0, 0), (-1, 0, 0), (0, 1, 0), (0, -1, 0), (0, 0, 1), (0, 0, -1),
            (1, 1, 0), (-1, -1, 0), (1, -1, 0), (-1, 1, 0), (1, 0, 1), (-1, 0, -1), (1, 0, -1), (-1, 0, 1),
            (0, 1, 1), (0, -1, -1), (0, 1, -1), (0, -1, 1))
WEIGHT = (1.0 / 3.0,) + (1.0 / 18.0,) * 6 + (1.0 / 36.0,) * 12
KERNEL = (0.25, 0.5, 0.25)
RELAX = 0.8


def along(vector, direction):
    total = jnp.zeros_like(vector[0])
    for axis_pos in range(3):
        if direction[axis_pos] == 1:
            total = total + vector[axis_pos]
        elif direction[axis_pos] == -1:
            total = total - vector[axis_pos]
    return total


def moments(fields):
    density = fields[0]
    for index in range(1, 19):
        density = density + fields[index]
    rows = []
    for axis_pos in range(3):
        total = jnp.zeros_like(density)
        for index in range(19):
            if VELOCITY[index][axis_pos] == 1:
                total = total + fields[index]
            elif VELOCITY[index][axis_pos] == -1:
                total = total - fields[index]
        rows.append(total)
    return density, jnp.stack(rows)


def collide(fields, density, momentum, field):
    velocity = (momentum + 0.5 * field) / density
    square = velocity[0] * velocity[0] + velocity[1] * velocity[1] + velocity[2] * velocity[2]
    work = velocity[0] * field[0] + velocity[1] * field[1] + velocity[2] * field[2]
    outputs = []
    for index in range(19):
        proj_u = along(velocity, VELOCITY[index])
        proj_f = along(field, VELOCITY[index])
        equil = WEIGHT[index] * density * (1.0 + 3.0 * proj_u + 4.5 * proj_u * proj_u - 1.5 * square)
        source = (1.0 - 0.5 / RELAX) * WEIGHT[index] * (3.0 * (proj_f - work) + 9.0 * proj_u * proj_f)
        outputs.append(fields[index] - (fields[index] - equil) / RELAX + source)
    return jnp.stack(outputs)


def reference(populations, panels, modal_vel, marker_x, marker_y, marker_z, marker_riser):
    size_x = populations.shape[1]
    size_y = populations.shape[2]
    size_z = populations.shape[3]
    tiles_x, tiles_y, count = marker_x.shape
    read = jnp.stack([jnp.roll(populations[i], VELOCITY[i], axis=(0, 1, 2)) for i in range(19)])
    density, momentum = moments(read)
    fluid_vel = momentum / density
    targets = jnp.einsum("rcm,rmz->rcz", modal_vel.astype(jnp.float32), panels.astype(jnp.float32),
                         precision=lax.Precision.HIGHEST)
    tile_x = lax.broadcasted_iota(jnp.int32, marker_x.shape, 0)
    tile_y = lax.broadcasted_iota(jnp.int32, marker_x.shape, 1)
    glob_x = (tile_x * (size_x // tiles_x) + marker_x).reshape(-1)
    glob_y = (tile_y * (size_y // tiles_y) + marker_y).reshape(-1)
    glob_z = marker_z.reshape(-1)
    riser = marker_riser.reshape(-1)
    sampled = jnp.zeros((3, glob_x.shape[0]), jnp.float32)
    for shift_a in range(3):
        for shift_b in range(3):
            index_x = (glob_x + shift_a - 1) % size_x
            index_y = (glob_y + shift_b - 1) % size_y
            sampled = sampled + (KERNEL[shift_a] * KERNEL[shift_b]) * fluid_vel[:, index_x, index_y, glob_z]
    chosen = targets[riser, :, glob_z].T
    wanted = jnp.concatenate([chosen, jnp.zeros((1, glob_x.shape[0]), jnp.float32)], axis=0)
    force = 2.0 * (wanted - sampled)
    field = jnp.zeros((3, size_x, size_y, size_z), jnp.float32)
    for shift_a in range(3):
        for shift_b in range(3):
            index_x = (glob_x + shift_a - 1) % size_x
            index_y = (glob_y + shift_b - 1) % size_y
            field = field.at[:, index_x, index_y, glob_z].add((KERNEL[shift_a] * KERNEL[shift_b]) * force)
    next_populations = collide(read, density, momentum, field)
    marker_force = force.reshape(3, tiles_x, tiles_y, count).transpose(1, 2, 0, 3)
    return next_populations, marker_force, field
```

```python
import jax
import jax.numpy as jnp
from jax import lax
from jax.experimental import pallas as pl
from jax.experimental.pallas import tpu as pltpu
from jax.sharding import PartitionSpec as P

VELOCITY = (
    (0, 0, 0),
    (1, 0, 0),
    (-1, 0, 0),
    (0, 1, 0),
    (0, -1, 0),
    (0, 0, 1),
    (0, 0, -1),
    (1, 1, 0),
    (-1, -1, 0),
    (1, -1, 0),
    (-1, 1, 0),
    (1, 0, 1),
    (-1, 0, -1),
    (1, 0, -1),
    (-1, 0, 1),
    (0, 1, 1),
    (0, -1, -1),
    (0, 1, -1),
    (0, -1, 1),
)
WEIGHT = (1.0 / 3.0,) + (1.0 / 18.0,) * 6 + (1.0 / 36.0,) * 12
RELAX = 0.8
CELLS = 16
DEPTH = 128
MARKS = 512
RISERS = 64
FRAME = 24
WIDE = CELLS + 6


def slabs(axis, toward):
    order = []
    for layer in (1, 2, 3):
        for index in range(19):
            if VELOCITY[index][axis] * toward >= layer - 2:
                order.append((layer, index))
    return order


ORDER = {(axis, toward): slabs(axis, toward) for axis in (0, 1) for toward in (1, -1)}
PLACE = {key: {slab: k for k, slab in enumerate(order)} for key, order in ORDER.items()}
SLABS = len(ORDER[0, 1])
INWARD = {toward: [i for i in range(19) if VELOCITY[i][1] == toward] for toward in (1, -1)}


def near(layer, toward):
    return CELLS - layer if toward == 1 else layer - 1


def encode(value, index):
    return (value - WEIGHT[index]).astype(jnp.bfloat16)


def decode(value, index):
    return value.astype(jnp.float32) + WEIGHT[index]


def split(value):
    high = value.astype(jnp.bfloat16)
    low = (value - high.astype(jnp.float32)).astype(jnp.bfloat16)
    return high, low


def pack_faces(cells, marks, panel, modal, xup, xdown, yup, ydown, rows):
    for out, toward in ((xup, 1), (xdown, -1)):
        for k, (layer, index) in enumerate(ORDER[0, toward]):
            first = near(layer, toward) * CELLS
            out[k] = encode(cells[index, first : first + CELLS, :], index)
        out[SLABS] = marks[...].astype(jnp.bfloat16)
    for out, toward in ((yup, 1), (ydown, -1)):
        for k, (layer, index) in enumerate(ORDER[1, toward]):
            row = near(layer, toward)
            out[k] = encode(cells[index, pl.ds(row, CELLS, stride=CELLS), :], index)
        out[SLABS] = marks[...].astype(jnp.bfloat16)
    product = lax.dot_general(
        panel[...], modal[...], (((1,), (1,)), ((), ())), preferred_element_type=jnp.float32
    )
    mine = lax.broadcasted_iota(jnp.int32, product.shape, 0) == (
        lax.broadcasted_iota(jnp.int32, product.shape, 1) & (RISERS - 1)
    )
    row = jnp.sum(jnp.where(mine, product, 0.0), axis=0, keepdims=True)
    rows[...] = jnp.broadcast_to(row, rows.shape)


def pack_corners(xlow, xhigh, yup, ydown, low, high):
    low[...] = xlow[...].astype(jnp.float32)
    high[...] = xhigh[...].astype(jnp.float32)
    place = lax.broadcasted_iota(jnp.int32, (8, DEPTH), 0)
    for out, toward in ((yup, 1), (ydown, -1)):
        for k, (layer, index) in enumerate(ORDER[1, toward]):
            row = near(layer, toward)
            tile = jnp.zeros((8, DEPTH), jnp.float32)
            for depth in (1, 2, 3):
                for source, side, at in ((high, -1, depth - 1), (low, 1, 8 - depth)):
                    slot = PLACE[0, side].get((depth, index))
                    if slot is not None:
                        tile = jnp.where(place == at, source[slot, row : row + 1, :], tile)
            out[k] = tile.astype(jnp.bfloat16)
        for n, source in enumerate((low, high)):
            for half in range(2):
                out[SLABS + 2 * n + half] = source[SLABS, 8 * half : 8 * half + 8, :].astype(
                    jnp.bfloat16
                )


def moments(reads):
    density = None
    momentum = [None, None, None]
    for index, value in enumerate(reads):
        density = value if density is None else density + value
        for axis in range(3):
            sign = VELOCITY[index][axis]
            if sign == 1:
                momentum[axis] = value if momentum[axis] is None else momentum[axis] + value
            elif sign == -1:
                momentum[axis] = -value if momentum[axis] is None else momentum[axis] - value
    return density, momentum


def along(vector, direction):
    total = None
    for axis in range(3):
        if direction[axis] == 1:
            total = vector[axis] if total is None else total + vector[axis]
        elif direction[axis] == -1:
            total = -vector[axis] if total is None else total - vector[axis]
    return total


def spin(value, shift, axis):
    return pltpu.roll(value, shift % value.shape[axis], axis) if shift else value


def step_kernel(
    cells,
    xlow,
    xhigh,
    ylow,
    yhigh,
    clow,
    chigh,
    sentlow,
    senthigh,
    sentclow,
    sentchigh,
    marks,
    table,
    nxt,
    push,
    field,
    wide,
    edge,
    strip,
    lines,
    vel,
    tall,
    smooth,
    dens,
    impulse,
    sem,
):
    inner = pltpu.make_async_copy(cells, wide.at[:, pl.ds(3 * CELLS, CELLS * CELLS), :], sem)
    inner.start()
    f32 = jnp.float32
    for message, toward in ((xlow, 1), (xhigh, -1)):
        for k, (layer, index) in enumerate(ORDER[0, toward]):
            column = 3 - layer if toward == 1 else 2 + CELLS + layer
            wide[index, column * CELLS : (column + 1) * CELLS, :] = decode(message[k], index)

    def frame(face, corner, k, index):
        return jnp.concatenate([decode(face[k], index), decode(corner[k], index)], axis=0)

    sides = (
        (1, ylow, clow, sentlow, sentclow),
        (-1, yhigh, chigh, senthigh, sentchigh),
    )
    for s, (toward, face, corner, ownface, owncorner) in enumerate(sides):
        for n, index in enumerate(INWARD[toward]):
            edge[s, n] = frame(face, corner, PLACE[1, toward][1, index], index)
        for layer in (1, 2):

            def reads():
                for index in range(19):
                    cx, cy, cz = VELOCITY[index]
                    source = layer + toward * cy
                    if source == 0:
                        value = frame(ownface, owncorner, PLACE[1, -toward][1, index], index)
                    else:
                        value = frame(face, corner, PLACE[1, toward][source, index], index)
                    yield spin(spin(value, cx, 0), cz, 1)

            density, momentum = moments(reads())
            for axis in range(3):
                strip[s, layer - 1, axis] = momentum[axis] / density

    row = lax.broadcasted_iota(jnp.int32, (CELLS, DEPTH), 0)
    inner.wait()

    def column(j, keep):
        def reads():
            for index in range(19):
                cx, cy, cz = VELOCITY[index]
                at = j + 1 - cx
                value = wide[index, pl.ds(pl.multiple_of(at * CELLS, CELLS), CELLS), :]
                if cy:
                    s = 0 if cy == 1 else 1
                    n = INWARD[cy].index(index)
                    line = edge[s, n, pl.ds(lax.rem(at + 21, FRAME), 1), :]
                    value = jnp.where(row == (0 if cy == 1 else CELLS - 1), line, spin(value, cy, 0))
                value = spin(value, cz, 1)
                if keep:
                    nxt[index, pl.ds(pl.multiple_of((j - 2) * CELLS, CELLS), CELLS), :] = value
                yield value

        density, momentum = moments(reads())
        if keep:
            dens[0, j - 2] = density
        for axis in range(3):
            speed = momentum[axis] / density
            if keep:
                dens[1 + axis, j - 2] = momentum[axis]
            vel[axis, j] = speed
            at = pl.ds(lax.rem(j + 22, FRAME), 1)
            lines[0, axis, at, :] = speed[0:1]
            lines[1, axis, at, :] = speed[CELLS - 1 : CELLS]

    for j in (0, 1, 18, 19):
        column(jnp.int32(j), False)

    @pl.loop(2, 18)
    def _(j):
        column(j, True)

    @pl.loop(0, 20)
    def _(j):
        at = pl.ds(lax.rem(j + 22, FRAME), 1)
        for axis in range(3):
            value = vel[axis, j]
            before = jnp.where(row == 0, strip[0, 0, axis, at, :], spin(value, 1, 0))
            after = jnp.where(row == CELLS - 1, strip[1, 0, axis, at, :], spin(value, -1, 0))
            tall[axis, j] = 0.5 * value + 0.25 * (before + after)

    @pl.loop(0, 18)
    def _(j):
        for axis in range(3):
            smooth[axis, j] = 0.5 * tall[axis, j + 1] + 0.25 * (tall[axis, j] + tall[axis, j + 2])

    place = lax.broadcasted_iota(jnp.int32, (FRAME, DEPTH), 0)
    inside = (place <= CELLS) | (place == FRAME - 1)
    rim = []
    for s in range(2):
        for axis in range(3):
            value = 0.5 * strip[s, 0, axis] + 0.25 * (strip[s, 1, axis] + lines[s, axis])
            value = 0.5 * value + 0.25 * (spin(value, 1, 0) + spin(value, -1, 0))
            rim.append(jnp.where(inside, value, 0.0))

    goal = split(table[...].T)
    goal = jnp.concatenate(goal, axis=1)

    def group(slab, chunks):
        return [
            jnp.concatenate(
                [slab[attr * 4 + n : attr * 4 + n + 1, :] for n in range(chunks)], axis=1
            )
            for attr in range(4)
        ]

    def hot(position, count):
        shape = (count, position.shape[1])
        return lax.broadcasted_iota(jnp.int32, shape, 0).astype(f32) == position

    def force_of(velocity, weight, z, riser):
        at_z = jnp.where(hot(z, DEPTH), 1.0, 0.0).astype(jnp.bfloat16)
        twice = jnp.concatenate([at_z, at_z], axis=0)
        picked = jnp.dot(goal, twice, preferred_element_type=f32)
        at_riser = hot(riser, RISERS)
        out = []
        for axis in range(3):
            both = jnp.concatenate(split(velocity[axis]), axis=1)
            speed = jnp.dot(both, twice, preferred_element_type=f32)
            sampled = jnp.sum(jnp.where(weight, speed, 0.0), axis=0, keepdims=True)
            if axis < 2:
                some = picked[axis * RISERS : (axis + 1) * RISERS]
                wanted = jnp.sum(jnp.where(at_riser, some, 0.0), axis=0, keepdims=True)
                out.append(2.0 * (wanted - sampled))
            else:
                out.append(-2.0 * sampled)
        return at_z, out

    contract = (((1,), (1,)), ((), ()))

    def spread(weight, at_z, force):
        parts = []
        for axis in range(3):
            parts.append(jnp.where(weight, force[axis], 0.0))
        high, low = split(jnp.concatenate(parts, axis=0))
        both = jnp.concatenate([high, low], axis=1)
        twice = jnp.concatenate([at_z, at_z], axis=1)
        return lax.dot_general(both, twice, contract, preferred_element_type=f32)

    mx, my, mz, riser = group(marks[...], 4)
    weight = hot(mx * CELLS + my, CELLS * CELLS)
    velocity = [smooth[axis, 1 : CELLS + 1].reshape(CELLS * CELLS, DEPTH) for axis in range(3)]
    at_z, force = force_of(velocity, weight, mz, riser)
    for axis in range(3):
        push[axis : axis + 1, :] = force[axis]
    at_cell = jnp.where(weight, 1.0, 0.0).astype(jnp.bfloat16)
    where_z = hot(mz, DEPTH)
    for axis in range(3):
        high, low = split(jnp.where(where_z, force[axis], 0.0))
        got = lax.dot_general(at_cell, high, contract, preferred_element_type=f32)
        got = got + lax.dot_general(at_cell, low, contract, preferred_element_type=f32)
        impulse[axis, 1 : CELLS + 1] = got.reshape(CELLS, CELLS, DEPTH)
    for message, at, spot in ((xlow, CELLS - 1, 0), (xhigh, 0, CELLS + 1)):
        mx, my, mz, riser = group(message[SLABS].astype(f32), 4)
        weight = hot(jnp.where(mx == at, my, -1.0), CELLS)
        at_z, force = force_of([smooth[axis, spot] for axis in range(3)], weight, mz, riser)
        got = spread(weight, at_z, force)
        for axis in range(3):
            impulse[axis, spot] = got[axis * CELLS : (axis + 1) * CELLS]
    for s, (face, corner, at) in enumerate(((ylow, clow, CELLS - 1), (yhigh, chigh, 0))):
        tiles = [face[SLABS].astype(f32)]
        for n in range(2):
            tiles.append(
                jnp.concatenate(
                    [corner[SLABS + 2 * n + half].astype(f32) for half in range(2)], axis=0
                )
            )
        found = [group(tile, 4) for tile in tiles]
        spots = []
        for (mx, my, _, _), shift in zip(found, (0, 8, CELLS)):
            spot = mx + shift
            keep = my == at
            if shift == 8:
                keep = keep & (mx == CELLS - 1)
            elif shift == CELLS:
                keep = keep & (mx == 0)
            spots.append(jnp.where(keep, spot, -1.0))
        weight = hot(jnp.concatenate(spots, axis=1), FRAME)
        mz = jnp.concatenate([g[2] for g in found], axis=1)
        riser = jnp.concatenate([g[3] for g in found], axis=1)
        at_z, force = force_of(rim[3 * s : 3 * s + 3], weight, mz, riser)
        got = spread(weight, at_z, force)
        for axis in range(3):
            lines[s, axis] = got[axis * FRAME : (axis + 1) * FRAME]

    @pl.loop(0, 18)
    def _(j):
        at = pl.ds(lax.rem(j + 23, FRAME), 1)
        for axis in range(3):
            value = impulse[axis, j]
            before = jnp.where(row == 0, lines[0, axis, at, :], spin(value, 1, 0))
            after = jnp.where(row == CELLS - 1, lines[1, axis, at, :], spin(value, -1, 0))
            tall[axis, j] = 0.5 * value + 0.25 * (before + after)

    @pl.loop(0, CELLS)
    def _(x):
        density = dens[0, x]
        own = []
        speed = []
        for axis in range(3):
            value = 0.5 * tall[axis, x + 1] + 0.25 * (tall[axis, x] + tall[axis, x + 2])
            field[axis, x] = value
            own.append(value)
            speed.append((dens[1 + axis, x] + 0.5 * value) / density)
        square = speed[0] * speed[0] + speed[1] * speed[1] + speed[2] * speed[2]
        work = speed[0] * own[0] + speed[1] * own[1] + speed[2] * own[2]
        at = pl.ds(pl.multiple_of(x * CELLS, CELLS), CELLS)
        for index in range(19):
            value = nxt[index, at, :]
            if index:
                proj_u = along(speed, VELOCITY[index])
                proj_f = along(own, VELOCITY[index])
                bracket = 1.0 + 3.0 * proj_u + 4.5 * proj_u * proj_u - 1.5 * square
                pull = 3.0 * (proj_f - work) + 9.0 * proj_u * proj_f
            else:
                bracket = 1.0 - 1.5 * square
                pull = -3.0 * work
            equil = WEIGHT[index] * density * bracket
            source = (1.0 - 0.5 / RELAX) * WEIGHT[index] * pull
            nxt[index, at, :] = value - (value - equil) / RELAX + source


def on_device(populations, panels, modal_vel, marker_x, marker_y, marker_z, marker_riser):
    f32, bf16 = jnp.float32, jnp.bfloat16
    shape = jax.ShapeDtypeStruct
    gx, gy = lax.axis_size("gx"), lax.axis_size("gy")
    devices = gx * gy
    cells = populations.reshape(19, CELLS * CELLS, DEPTH)
    marks = jnp.concatenate(
        [m.reshape(4, 128) for m in (marker_x, marker_y, marker_z, marker_riser)], axis=0
    ).astype(f32)
    modal = modal_vel.transpose(1, 0, 2).reshape(2 * RISERS, -1)
    panel = panels.reshape(RISERS, -1)
    vmem = pl.BlockSpec(memory_space=pltpu.VMEM)
    face = shape((SLABS + 1, CELLS, DEPTH), bf16)
    corner = shape((SLABS + 4, 8, DEPTH), bf16)
    xup, xdown, yup, ydown, rows = pl.pallas_call(
        pack_faces,
        out_shape=(face, face, face, face, shape((devices, 128), f32)),
        in_specs=[vmem] * 4,
        out_specs=(vmem,) * 5,
        name="pack_faces",
    )(cells, marks, panel, modal)

    def ring(axis, toward):
        size = lax.axis_size(axis)
        return [(i, (i + toward) % size) for i in range(size)]

    xlow = lax.ppermute(xup, "gx", ring("gx", 1))
    xhigh = lax.ppermute(xdown, "gx", ring("gx", -1))
    ylow = lax.ppermute(yup, "gy", ring("gy", 1))
    yhigh = lax.ppermute(ydown, "gy", ring("gy", -1))
    table = lax.all_to_all(rows, ("gx", "gy"), 0, 0, tiled=True)
    cup, cdown = pl.pallas_call(
        pack_corners,
        out_shape=(corner, corner),
        in_specs=[vmem] * 2,
        out_specs=(vmem,) * 2,
        scratch_shapes=[pltpu.VMEM((SLABS + 1, CELLS, DEPTH), f32)] * 2,
        name="pack_corners",
    )(xlow, xhigh)
    clow = lax.ppermute(cup, "gy", ring("gy", 1))
    chigh = lax.ppermute(cdown, "gy", ring("gy", -1))
    nxt, push, field = pl.pallas_call(
        step_kernel,
        out_shape=(
            shape((19, CELLS * CELLS, DEPTH), f32),
            shape((3, MARKS), f32),
            shape((3, CELLS, CELLS, DEPTH), f32),
        ),
        in_specs=[pl.BlockSpec(memory_space=pl.ANY)] + [vmem] * 12,
        out_specs=(vmem,) * 3,
        scratch_shapes=[
            pltpu.VMEM((19, WIDE * CELLS, DEPTH), f32),
            pltpu.VMEM((2, 5, FRAME, DEPTH), f32),
            pltpu.VMEM((2, 2, 3, FRAME, DEPTH), f32),
            pltpu.VMEM((2, 3, FRAME, DEPTH), f32),
            pltpu.VMEM((3, 20, CELLS, DEPTH), f32),
            pltpu.VMEM((3, 20, CELLS, DEPTH), f32),
            pltpu.VMEM((3, 18, CELLS, DEPTH), f32),
            pltpu.VMEM((4, CELLS, CELLS, DEPTH), f32),
            pltpu.VMEM((3, 18, CELLS, DEPTH), f32),
            pltpu.SemaphoreType.DMA,
        ],
        name="step_kernel",
    )(cells, xlow, xhigh, ylow, yhigh, clow, chigh, ydown, yup, cdown, cup, marks, table)
    return (
        nxt.reshape(19, CELLS, CELLS, DEPTH),
        push[None, None],
        field,
    )


def solution(mesh):
    in_specs = (
        P(None, "gx", "gy", None),
        P(None, None, ("gx", "gy")),
        P(),
        P("gx", "gy", None),
        P("gx", "gy", None),
        P("gx", "gy", None),
        P("gx", "gy", None),
    )
    out_specs = (P(None, "gx", "gy", None), P("gx", "gy", None, None), P(None, "gx", "gy", None))
    return jax.shard_map(
        on_device, mesh=mesh, in_specs=in_specs, out_specs=out_specs, check_vma=False
    )
```

```python
import jax
import jax.numpy as jnp
from jax import lax
from jax.experimental import pallas as pl
from jax.experimental.pallas import tpu as pltpu
from jax.sharding import PartitionSpec as P

VELOCITY = (
    (0, 0, 0),
    (1, 0, 0),
    (-1, 0, 0),
    (0, 1, 0),
    (0, -1, 0),
    (0, 0, 1),
    (0, 0, -1),
    (1, 1, 0),
    (-1, -1, 0),
    (1, -1, 0),
    (-1, 1, 0),
    (1, 0, 1),
    (-1, 0, -1),
    (1, 0, -1),
    (-1, 0, 1),
    (0, 1, 1),
    (0, -1, -1),
    (0, 1, -1),
    (0, -1, 1),
)
WEIGHT = (1.0 / 3.0,) + (1.0 / 18.0,) * 6 + (1.0 / 36.0,) * 12
RELAX = 0.8
CELLS = 16
DEPTH = 128
MARKS = 512
RISERS = 64
FRAME = 24


def slabs(axis, toward):
    order = []
    for layer in (1, 2, 3):
        for index in range(19):
            if VELOCITY[index][axis] * toward >= layer - 2:
                order.append((layer, index))
    return order


ORDER = {(axis, toward): slabs(axis, toward) for axis in (0, 1) for toward in (1, -1)}
PLACE = {key: {slab: k for k, slab in enumerate(order)} for key, order in ORDER.items()}
SLABS = len(ORDER[0, 1])
INWARD = {toward: [i for i in range(19) if VELOCITY[i][1] == toward] for toward in (1, -1)}


def near(layer, toward):
    return CELLS - layer if toward == 1 else layer - 1


def encode(value, index):
    return (value - WEIGHT[index]).astype(jnp.bfloat16)


def decode(value, index):
    return value.astype(jnp.float32) + WEIGHT[index]


def split(value):
    high = value.astype(jnp.bfloat16)
    low = (value - high.astype(jnp.float32)).astype(jnp.bfloat16)
    return high, low


def pack_faces(
    cells_far,
    mx_far,
    my_far,
    mz_far,
    riser_far,
    panel_far,
    modal_far,
    xup,
    xdown,
    yup,
    ydown,
    rows,
    cells,
    mx,
    my,
    mz,
    riser,
    panel,
    modal,
    marks,
    pairs,
    sems,
):
    copies = [
        pltpu.make_async_copy(far, here, sems.at[n])
        for n, (far, here) in enumerate(
            (
                (modal_far, modal),
                (panel_far, panel),
                (mx_far, mx),
                (my_far, my),
                (mz_far, mz),
                (riser_far, riser),
                (cells_far, cells),
            )
        )
    ]
    for copy in copies:
        copy.start()
    for copy in copies[:6]:
        copy.wait()
    for attr, source in enumerate((mx, my, mz, riser)):
        for n in range(4):
            marks[attr * 4 + n : attr * 4 + n + 1, :] = source[:, n * 128 : (n + 1) * 128].astype(
                jnp.float32
            )
    for n in range(RISERS):
        both = modal[n].astype(jnp.float32)
        for d in range(2):
            pairs[d * RISERS + n : d * RISERS + n + 1, :] = both[d : d + 1]
    product = lax.dot_general(
        panel[...],
        pairs[...].astype(jnp.bfloat16),
        (((1,), (1,)), ((), ())),
        preferred_element_type=jnp.float32,
    )
    mine = lax.broadcasted_iota(jnp.int32, product.shape, 0) == (
        lax.broadcasted_iota(jnp.int32, product.shape, 1) & (RISERS - 1)
    )
    row = jnp.sum(jnp.where(mine, product, 0.0), axis=0, keepdims=True)
    rows[...] = jnp.broadcast_to(row, rows.shape)
    copies[6].wait()
    for out, toward in ((xup, 1), (xdown, -1)):
        for k, (layer, index) in enumerate(ORDER[0, toward]):
            first = near(layer, toward) * CELLS
            out[k] = encode(cells[index, first : first + CELLS, :], index)
        out[SLABS] = marks[...].astype(jnp.bfloat16)
    for out, toward in ((yup, 1), (ydown, -1)):
        for k, (layer, index) in enumerate(ORDER[1, toward]):
            row = near(layer, toward)
            out[k] = encode(cells[index, pl.ds(row, CELLS, stride=CELLS), :], index)
        out[SLABS] = marks[...].astype(jnp.bfloat16)


def pack_corners(xlow, xhigh, yup, ydown, low, high):
    low[...] = xlow[...].astype(jnp.float32)
    high[...] = xhigh[...].astype(jnp.float32)
    place = lax.broadcasted_iota(jnp.int32, (8, DEPTH), 0)
    for out, toward in ((yup, 1), (ydown, -1)):
        for k, (layer, index) in enumerate(ORDER[1, toward]):
            row = near(layer, toward)
            tile = jnp.zeros((8, DEPTH), jnp.float32)
            for depth in (1, 2, 3):
                for source, side, at in ((high, -1, depth - 1), (low, 1, 8 - depth)):
                    slot = PLACE[0, side].get((depth, index))
                    if slot is not None:
                        tile = jnp.where(place == at, source[slot, row : row + 1, :], tile)
            out[k] = tile.astype(jnp.bfloat16)
        for n, source in enumerate((low, high)):
            for half in range(2):
                out[SLABS + 2 * n + half] = source[SLABS, 8 * half : 8 * half + 8, :].astype(
                    jnp.bfloat16
                )


def moments(reads):
    density = None
    momentum = [None, None, None]
    for index, value in enumerate(reads):
        density = value if density is None else density + value
        for axis in range(3):
            sign = VELOCITY[index][axis]
            if sign == 1:
                momentum[axis] = value if momentum[axis] is None else momentum[axis] + value
            elif sign == -1:
                momentum[axis] = -value if momentum[axis] is None else momentum[axis] - value
    return density, momentum


def along(vector, direction):
    total = None
    for axis in range(3):
        if direction[axis] == 1:
            total = vector[axis] if total is None else total + vector[axis]
        elif direction[axis] == -1:
            total = -vector[axis] if total is None else total - vector[axis]
    return total


def spin(value, shift, axis):
    return pltpu.roll(value, shift % value.shape[axis], axis) if shift else value


def step_kernel(
    cells,
    xlow,
    xhigh,
    ylow,
    yhigh,
    clow,
    chigh,
    own_x,
    own_y,
    own_z,
    own_riser,
    table,
    nxt,
    push,
    field,
    wide,
    edge,
    strip,
    lines,
    vel,
    tall,
    smooth,
    dens,
    impulse,
    sem,
):
    inner = pltpu.make_async_copy(cells, wide.at[:, pl.ds(0, CELLS * CELLS), :], sem)
    inner.start()
    f32 = jnp.float32
    for message, toward in ((xlow, 1), (xhigh, -1)):
        for k, (layer, index) in enumerate(ORDER[0, toward]):
            column = FRAME - layer if toward == 1 else CELLS - 1 + layer
            wide[index, column * CELLS : (column + 1) * CELLS, :] = decode(message[k], index)

    def frame(face, corner, k, index):
        return jnp.concatenate([decode(face[k], index), decode(corner[k], index)], axis=0)

    inner.wait()

    for s, (toward, face, corner) in enumerate(((1, ylow, clow), (-1, yhigh, chigh))):
        first = 0 if toward == 1 else CELLS - 1
        for n, index in enumerate(INWARD[toward]):
            edge[s, n] = frame(face, corner, PLACE[1, toward][1, index], index)
        for layer in (1, 2):

            def reads():
                for index in range(19):
                    cx, cy, cz = VELOCITY[index]
                    source = layer + toward * cy
                    if source == 0:
                        value = wide[index, pl.ds(first, FRAME, stride=CELLS), :]
                    else:
                        value = frame(face, corner, PLACE[1, toward][source, index], index)
                    yield spin(spin(value, cx, 0), cz, 1)

            density, momentum = moments(reads())
            for axis in range(3):
                strip[s, layer - 1, axis] = momentum[axis] / density

    row = lax.broadcasted_iota(jnp.int32, (CELLS, DEPTH), 0)

    def column(j, keep):
        def reads():
            for index in range(19):
                cx, cy, cz = VELOCITY[index]
                at = lax.rem(j + (FRAME - 2) - cx, FRAME)
                value = wide[index, pl.ds(pl.multiple_of(at * CELLS, CELLS), CELLS), :]
                if cy:
                    s = 0 if cy == 1 else 1
                    n = INWARD[cy].index(index)
                    line = edge[s, n, pl.ds(at, 1), :]
                    value = jnp.where(row == (0 if cy == 1 else CELLS - 1), line, spin(value, cy, 0))
                value = spin(value, cz, 1)
                if keep:
                    nxt[index, pl.ds(pl.multiple_of((j - 2) * CELLS, CELLS), CELLS), :] = value
                yield value

        density, momentum = moments(reads())
        if keep:
            dens[0, j - 2] = density
        for axis in range(3):
            speed = momentum[axis] / density
            if keep:
                dens[1 + axis, j - 2] = momentum[axis]
            vel[axis, j] = speed
            at = pl.ds(lax.rem(j + 22, FRAME), 1)
            lines[0, axis, at, :] = speed[0:1]
            lines[1, axis, at, :] = speed[CELLS - 1 : CELLS]

    for j in (0, 1, 18, 19):
        column(jnp.int32(j), False)

    @pl.loop(2, 18)
    def _(j):
        column(j, True)

    @pl.loop(0, 20)
    def _(j):
        at = pl.ds(lax.rem(j + 22, FRAME), 1)
        for axis in range(3):
            value = vel[axis, j]
            before = jnp.where(row == 0, strip[0, 0, axis, at, :], spin(value, 1, 0))
            after = jnp.where(row == CELLS - 1, strip[1, 0, axis, at, :], spin(value, -1, 0))
            tall[axis, j] = 0.5 * value + 0.25 * (before + after)

    @pl.loop(0, 18)
    def _(j):
        for axis in range(3):
            smooth[axis, j] = 0.5 * tall[axis, j + 1] + 0.25 * (tall[axis, j] + tall[axis, j + 2])

    place = lax.broadcasted_iota(jnp.int32, (FRAME, DEPTH), 0)
    inside = (place <= CELLS) | (place == FRAME - 1)
    rim = []
    for s in range(2):
        for axis in range(3):
            value = 0.5 * strip[s, 0, axis] + 0.25 * (strip[s, 1, axis] + lines[s, axis])
            value = 0.5 * value + 0.25 * (spin(value, 1, 0) + spin(value, -1, 0))
            rim.append(jnp.where(inside, value, 0.0))

    goal = split(table[...].T)
    goal = jnp.concatenate(goal, axis=1)

    def group(slab, chunks):
        return [
            jnp.concatenate(
                [slab[attr * 4 + n : attr * 4 + n + 1, :] for n in range(chunks)], axis=1
            )
            for attr in range(4)
        ]

    def hot(position, count):
        shape = (count, position.shape[1])
        return lax.broadcasted_iota(jnp.int32, shape, 0).astype(f32) == position

    def force_of(velocity, weight, z, riser):
        at_z = jnp.where(hot(z, DEPTH), 1.0, 0.0).astype(jnp.bfloat16)
        twice = jnp.concatenate([at_z, at_z], axis=0)
        picked = jnp.dot(goal, twice, preferred_element_type=f32)
        at_riser = hot(riser, RISERS)
        out = []
        for axis in range(3):
            both = jnp.concatenate(split(velocity[axis]), axis=1)
            speed = jnp.dot(both, twice, preferred_element_type=f32)
            sampled = jnp.sum(jnp.where(weight, speed, 0.0), axis=0, keepdims=True)
            if axis < 2:
                some = picked[axis * RISERS : (axis + 1) * RISERS]
                wanted = jnp.sum(jnp.where(at_riser, some, 0.0), axis=0, keepdims=True)
                out.append(2.0 * (wanted - sampled))
            else:
                out.append(-2.0 * sampled)
        return at_z, out

    contract = (((1,), (1,)), ((), ()))

    def spread(weight, at_z, force):
        parts = []
        for axis in range(3):
            parts.append(jnp.where(weight, force[axis], 0.0))
        high, low = split(jnp.concatenate(parts, axis=0))
        both = jnp.concatenate([high, low], axis=1)
        twice = jnp.concatenate([at_z, at_z], axis=1)
        return lax.dot_general(both, twice, contract, preferred_element_type=f32)

    mx, my, mz, riser = (m[...].astype(f32) for m in (own_x, own_y, own_z, own_riser))
    weight = hot(mx * CELLS + my, CELLS * CELLS)
    velocity = [smooth[axis, 1 : CELLS + 1].reshape(CELLS * CELLS, DEPTH) for axis in range(3)]
    at_z, force = force_of(velocity, weight, mz, riser)
    for axis in range(3):
        push[axis] = force[axis]
    at_cell = jnp.where(weight, 1.0, 0.0).astype(jnp.bfloat16)
    where_z = hot(mz, DEPTH)
    for axis in range(3):
        high, low = split(jnp.where(where_z, force[axis], 0.0))
        got = lax.dot_general(at_cell, high, contract, preferred_element_type=f32)
        got = got + lax.dot_general(at_cell, low, contract, preferred_element_type=f32)
        impulse[axis, 1 : CELLS + 1] = got.reshape(CELLS, CELLS, DEPTH)
    for message, at, spot in ((xlow, CELLS - 1, 0), (xhigh, 0, CELLS + 1)):
        mx, my, mz, riser = group(message[SLABS].astype(f32), 4)
        weight = hot(jnp.where(mx == at, my, -1.0), CELLS)
        at_z, force = force_of([smooth[axis, spot] for axis in range(3)], weight, mz, riser)
        got = spread(weight, at_z, force)
        for axis in range(3):
            impulse[axis, spot] = got[axis * CELLS : (axis + 1) * CELLS]
    for s, (face, corner, at) in enumerate(((ylow, clow, CELLS - 1), (yhigh, chigh, 0))):
        tiles = [face[SLABS].astype(f32)]
        for n in range(2):
            tiles.append(
                jnp.concatenate(
                    [corner[SLABS + 2 * n + half].astype(f32) for half in range(2)], axis=0
                )
            )
        found = [group(tile, 4) for tile in tiles]
        spots = []
        for (mx, my, _, _), shift in zip(found, (0, 8, CELLS)):
            spot = mx + shift
            keep = my == at
            if shift == 8:
                keep = keep & (mx == CELLS - 1)
            elif shift == CELLS:
                keep = keep & (mx == 0)
            spots.append(jnp.where(keep, spot, -1.0))
        weight = hot(jnp.concatenate(spots, axis=1), FRAME)
        mz = jnp.concatenate([g[2] for g in found], axis=1)
        riser = jnp.concatenate([g[3] for g in found], axis=1)
        at_z, force = force_of(rim[3 * s : 3 * s + 3], weight, mz, riser)
        got = spread(weight, at_z, force)
        for axis in range(3):
            lines[s, axis] = got[axis * FRAME : (axis + 1) * FRAME]

    @pl.loop(0, 18)
    def _(j):
        at = pl.ds(lax.rem(j + 23, FRAME), 1)
        for axis in range(3):
            value = impulse[axis, j]
            before = jnp.where(row == 0, lines[0, axis, at, :], spin(value, 1, 0))
            after = jnp.where(row == CELLS - 1, lines[1, axis, at, :], spin(value, -1, 0))
            tall[axis, j] = 0.5 * value + 0.25 * (before + after)

    @pl.loop(0, CELLS)
    def _(x):
        density = dens[0, x]
        own = []
        speed = []
        for axis in range(3):
            value = 0.5 * tall[axis, x + 1] + 0.25 * (tall[axis, x] + tall[axis, x + 2])
            field[axis, x] = value
            own.append(value)
            speed.append((dens[1 + axis, x] + 0.5 * value) / density)
        square = speed[0] * speed[0] + speed[1] * speed[1] + speed[2] * speed[2]
        work = speed[0] * own[0] + speed[1] * own[1] + speed[2] * own[2]
        at = pl.ds(pl.multiple_of(x * CELLS, CELLS), CELLS)
        for index in range(19):
            value = nxt[index, at, :]
            if index:
                proj_u = along(speed, VELOCITY[index])
                proj_f = along(own, VELOCITY[index])
                bracket = 1.0 + 3.0 * proj_u + 4.5 * proj_u * proj_u - 1.5 * square
                pull = 3.0 * (proj_f - work) + 9.0 * proj_u * proj_f
            else:
                bracket = 1.0 - 1.5 * square
                pull = -3.0 * work
            equil = WEIGHT[index] * density * bracket
            source = (1.0 - 0.5 / RELAX) * WEIGHT[index] * pull
            nxt[index, at, :] = value - (value - equil) / RELAX + source


def on_device(populations, panels, modal_vel, marker_x, marker_y, marker_z, marker_riser):
    f32, bf16 = jnp.float32, jnp.bfloat16
    shape = jax.ShapeDtypeStruct
    devices = lax.axis_size("gx") * lax.axis_size("gy")
    cells = populations.reshape(19, CELLS * CELLS, DEPTH)
    marks = [m.reshape(1, MARKS) for m in (marker_x, marker_y, marker_z, marker_riser)]
    panel = panels.reshape(RISERS, -1)
    modes = panel.shape[1]
    vmem = pl.BlockSpec(memory_space=pltpu.VMEM)
    face = shape((SLABS + 1, CELLS, DEPTH), bf16)
    corner = shape((SLABS + 4, 8, DEPTH), bf16)

    def limit(mib):
        return pltpu.CompilerParams(vmem_limit_bytes=mib << 20)

    xup, xdown, yup, ydown, rows = pl.pallas_call(
        pack_faces,
        out_shape=(face, face, face, face, shape((devices, 128), f32)),
        in_specs=[pl.BlockSpec(memory_space=pl.ANY)] * 7,
        out_specs=(vmem,) * 5,
        scratch_shapes=[
            pltpu.VMEM(cells.shape, f32),
            *[pltpu.VMEM((1, MARKS), jnp.int32)] * 4,
            pltpu.VMEM(panel.shape, bf16),
            pltpu.VMEM(modal_vel.shape, bf16),
            pltpu.VMEM((16, DEPTH), f32),
            pltpu.VMEM((2 * RISERS, modes), f32),
            pltpu.SemaphoreType.DMA((7,)),
        ],
        name="pack_faces",
    )(cells, *marks, panel, modal_vel)

    def ring(axis, toward):
        size = lax.axis_size(axis)
        return [(i, (i + toward) % size) for i in range(size)]

    xlow = lax.ppermute(xup, "gx", ring("gx", 1))
    xhigh = lax.ppermute(xdown, "gx", ring("gx", -1))
    ylow = lax.ppermute(yup, "gy", ring("gy", 1))
    yhigh = lax.ppermute(ydown, "gy", ring("gy", -1))
    table = lax.all_to_all(rows, ("gx", "gy"), 0, 0, tiled=True)
    cup, cdown = pl.pallas_call(
        pack_corners,
        out_shape=(corner, corner),
        in_specs=[vmem] * 2,
        out_specs=(vmem,) * 2,
        scratch_shapes=[pltpu.VMEM((SLABS + 1, CELLS, DEPTH), f32)] * 2,
        compiler_params=limit(8),
        name="pack_corners",
    )(xlow, xhigh)
    clow = lax.ppermute(cup, "gy", ring("gy", 1))
    chigh = lax.ppermute(cdown, "gy", ring("gy", -1))
    nxt, push, field = pl.pallas_call(
        step_kernel,
        out_shape=(
            shape((19, CELLS * CELLS, DEPTH), f32),
            shape((3, 1, MARKS), f32),
            shape((3, CELLS, CELLS, DEPTH), f32),
        ),
        in_specs=[pl.BlockSpec(memory_space=pl.ANY)] + [vmem] * 11,
        out_specs=(vmem,) * 3,
        scratch_shapes=[
            pltpu.VMEM((19, FRAME * CELLS, DEPTH), f32),
            pltpu.VMEM((2, 5, FRAME, DEPTH), f32),
            pltpu.VMEM((2, 2, 3, FRAME, DEPTH), f32),
            pltpu.VMEM((2, 3, FRAME, DEPTH), f32),
            pltpu.VMEM((3, 20, CELLS, DEPTH), f32),
            pltpu.VMEM((3, 20, CELLS, DEPTH), f32),
            pltpu.VMEM((3, 18, CELLS, DEPTH), f32),
            pltpu.VMEM((4, CELLS, CELLS, DEPTH), f32),
            pltpu.VMEM((3, 18, CELLS, DEPTH), f32),
            pltpu.SemaphoreType.DMA,
        ],
        compiler_params=limit(32),
        name="step_kernel",
    )(cells, xlow, xhigh, ylow, yhigh, clow, chigh, *marks, table)
    return (
        nxt.reshape(19, CELLS, CELLS, DEPTH),
        push.transpose(1, 0, 2)[None],
        field,
    )


def solution(mesh):
    in_specs = (
        P(None, "gx", "gy", None),
        P(None, None, ("gx", "gy")),
        P(),
        P("gx", "gy", None),
        P("gx", "gy", None),
        P("gx", "gy", None),
        P("gx", "gy", None),
    )
    out_specs = (P(None, "gx", "gy", None), P("gx", "gy", None, None), P(None, "gx", "gy", None))
    return jax.shard_map(on_device, mesh=mesh, in_specs=in_specs, out_specs=out_specs, check_vma=False)
```

```python
import jax
import jax.numpy as jnp
from jax import lax
from jax.experimental import pallas as pl
from jax.experimental.pallas import tpu as pltpu
from jax.sharding import PartitionSpec as P

VELOCITY = (
    (0, 0, 0),
    (1, 0, 0),
    (-1, 0, 0),
    (0, 1, 0),
    (0, -1, 0),
    (0, 0, 1),
    (0, 0, -1),
    (1, 1, 0),
    (-1, -1, 0),
    (1, -1, 0),
    (-1, 1, 0),
    (1, 0, 1),
    (-1, 0, -1),
    (1, 0, -1),
    (-1, 0, 1),
    (0, 1, 1),
    (0, -1, -1),
    (0, 1, -1),
    (0, -1, 1),
)
WEIGHT = (1.0 / 3.0,) + (1.0 / 18.0,) * 6 + (1.0 / 36.0,) * 12
RELAX = 0.8
CELLS = 16
DEPTH = 128
MARKS = 512
RISERS = 64
FRAME = 24


def slabs(axis, toward):
    order = []
    for layer in (1, 2, 3):
        for index in range(19):
            if VELOCITY[index][axis] * toward >= layer - 2:
                order.append((layer, index))
    return order


ORDER = {(axis, toward): slabs(axis, toward) for axis in (0, 1) for toward in (1, -1)}
PLACE = {key: {slab: k for k, slab in enumerate(order)} for key, order in ORDER.items()}
SLABS = len(ORDER[0, 1])
INWARD = {toward: [i for i in range(19) if VELOCITY[i][1] == toward] for toward in (1, -1)}


def near(layer, toward):
    return CELLS - layer if toward == 1 else layer - 1


def encode(value, index):
    return (value - WEIGHT[index]).astype(jnp.bfloat16)


def decode(value, index):
    return value.astype(jnp.float32) + WEIGHT[index]


def split(value):
    high = value.astype(jnp.bfloat16)
    low = (value - high.astype(jnp.float32)).astype(jnp.bfloat16)
    return high, low


def pack_x(
    cells_far, mx_far, my_far, mz_far, riser_far, panel_far, modal_far,
    xup, xdown, rows,
    first, last, mx, my, mz, riser, panel, modal, marks, pairs, sems,
):
    span = 3 * CELLS
    copies = [
        pltpu.make_async_copy(far, here, sems.at[n])
        for n, (far, here) in enumerate(
            (
                (modal_far, modal),
                (panel_far, panel),
                (mx_far, mx),
                (my_far, my),
                (mz_far, mz),
                (riser_far, riser),
                (cells_far.at[:, pl.ds(0, span), :], first),
                (cells_far.at[:, pl.ds(CELLS * CELLS - span, span), :], last),
            )
        )
    ]
    for copy in copies:
        copy.start()
    for copy in copies[:6]:
        copy.wait()
    fill_marks(marks, (mx, my, mz, riser))
    for n in range(RISERS):
        both = modal[n].astype(jnp.float32)
        for d in range(2):
            pairs[d * RISERS + n : d * RISERS + n + 1, :] = both[d : d + 1]
    product = lax.dot_general(
        panel[...],
        pairs[...].astype(jnp.bfloat16),
        (((1,), (1,)), ((), ())),
        preferred_element_type=jnp.float32,
    )
    mine = lax.broadcasted_iota(jnp.int32, product.shape, 0) == (
        lax.broadcasted_iota(jnp.int32, product.shape, 1) & (RISERS - 1)
    )
    row = jnp.sum(jnp.where(mine, product, 0.0), axis=0, keepdims=True)
    rows[...] = jnp.broadcast_to(row, rows.shape)
    for copy in copies[6:]:
        copy.wait()
    for out, toward in ((xup, 1), (xdown, -1)):
        for k, (layer, index) in enumerate(ORDER[0, toward]):
            if toward == 1:
                value = last[index, (3 - layer) * CELLS : (4 - layer) * CELLS, :]
            else:
                value = first[index, (layer - 1) * CELLS : layer * CELLS, :]
            out[k] = encode(value, index)
        out[SLABS] = marks[...].astype(jnp.bfloat16)


def fill_marks(marks, sources):
    for attr, source in enumerate(sources):
        for n in range(4):
            marks[attr * 4 + n : attr * 4 + n + 1, :] = source[:, n * 128 : (n + 1) * 128].astype(
                jnp.float32
            )


def pack_y(cells, xlow, xhigh, mx, my, mz, riser, yup, ydown, low, high, marks):
    low[...] = xlow[...].astype(jnp.float32)
    high[...] = xhigh[...].astype(jnp.float32)
    fill_marks(marks, (mx, my, mz, riser))
    place = lax.broadcasted_iota(jnp.int32, (8, DEPTH), 0)
    none = jnp.zeros((8, DEPTH), jnp.float32)
    for out, toward in ((yup, 1), (ydown, -1)):
        for k, (layer, index) in enumerate(ORDER[1, toward]):
            row = near(layer, toward)
            tile = none
            for depth in (1, 2, 3):
                for source, side, at in ((high, -1, depth - 1), (low, 1, 8 - depth)):
                    slot = PLACE[0, side].get((depth, index))
                    if slot is not None:
                        tile = jnp.where(place == at, source[slot, row : row + 1, :], tile)
            own = cells[index, pl.ds(row, CELLS, stride=CELLS), :] - WEIGHT[index]
            out[k] = jnp.concatenate([own, tile], axis=0).astype(jnp.bfloat16)
        for n, source in enumerate((marks[...], low[SLABS], high[SLABS])):
            out[SLABS + n] = jnp.concatenate([source, none], axis=0).astype(jnp.bfloat16)


def moments(reads):
    density = None
    momentum = [None, None, None]
    for index, value in enumerate(reads):
        density = value if density is None else density + value
        for axis in range(3):
            sign = VELOCITY[index][axis]
            if sign == 1:
                momentum[axis] = value if momentum[axis] is None else momentum[axis] + value
            elif sign == -1:
                momentum[axis] = -value if momentum[axis] is None else momentum[axis] - value
    return density, momentum


def along(vector, direction):
    total = None
    for axis in range(3):
        if direction[axis] == 1:
            total = vector[axis] if total is None else total + vector[axis]
        elif direction[axis] == -1:
            total = -vector[axis] if total is None else total - vector[axis]
    return total


def spin(value, shift, axis):
    return pltpu.roll(value, shift % value.shape[axis], axis) if shift else value


def step_kernel(
    cells, xlow, xhigh, ylow, yhigh, own_x, own_y, own_z, own_riser, table,
    nxt_far, push, field_far,
    nxt, field, side, edge, strip, lines, vel, tall, smooth, dens, impulse, sems,
):
    f32, bf16 = jnp.float32, jnp.bfloat16

    def rows_of(column):
        return slice(column * CELLS, (column + 1) * CELLS)

    for message, toward in ((xlow, 1), (xhigh, -1)):
        for k, (layer, index) in enumerate(ORDER[0, toward]):
            column = 8 - layer if toward == 1 else layer - 1
            side[index, rows_of(column), :] = decode(message[k], index)

    for s, (toward, message) in enumerate(((1, ylow), (-1, yhigh))):
        first = 0 if toward == 1 else CELLS - 1
        for n, index in enumerate(INWARD[toward]):
            edge[s, n] = decode(message[PLACE[1, toward][1, index]], index)
        for layer in (1, 2):

            def reads():
                for index in range(19):
                    cx, cy, cz = VELOCITY[index]
                    source = layer + toward * cy
                    if source == 0:
                        value = jnp.concatenate(
                            [
                                cells[index, pl.ds(first, CELLS, stride=CELLS), :],
                                side[index, pl.ds(first, 8, stride=CELLS), :],
                            ],
                            axis=0,
                        )
                    elif source == 1 and cy == toward:
                        value = edge[s, INWARD[toward].index(index)]
                    else:
                        value = decode(message[PLACE[1, toward][source, index]], index)
                    yield spin(spin(value, cx, 0), cz, 1)

            density, momentum = moments(reads())
            for axis in range(3):
                strip[s, layer - 1, axis] = momentum[axis] / density

    row = lax.broadcasted_iota(jnp.int32, (CELLS, DEPTH), 0)

    def column(x, known, keep):
        def reads():
            for index in range(19):
                cx, cy, cz = VELOCITY[index]
                if known:
                    at = (x - cx) % FRAME
                    if at < CELLS:
                        value = cells[index, rows_of(at), :]
                    else:
                        value = side[index, rows_of(at - CELLS), :]
                else:
                    at = x - cx
                    value = cells[index, pl.ds(pl.multiple_of(at * CELLS, CELLS), CELLS), :]
                if cy:
                    s = 0 if cy == 1 else 1
                    line = edge[s, INWARD[cy].index(index), pl.ds(at, 1), :]
                    value = jnp.where(row == (0 if cy == 1 else CELLS - 1), line, spin(value, cy, 0))
                value = spin(value, cz, 1)
                if keep:
                    if known:
                        nxt[index, rows_of(x), :] = value
                    else:
                        nxt[index, pl.ds(pl.multiple_of(x * CELLS, CELLS), CELLS), :] = value
                yield value

        density, momentum = moments(reads())
        at = pl.ds(x % FRAME if known else x, 1)
        if keep:
            dens[0, x] = density
        for axis in range(3):
            speed = momentum[axis] / density
            if keep:
                dens[1 + axis, x] = momentum[axis]
            vel[axis, x + 2] = speed
            lines[0, axis, at, :] = speed[0:1]
            lines[1, axis, at, :] = speed[CELLS - 1 : CELLS]

    for x in (-2, -1, 0, CELLS - 1, CELLS, CELLS + 1):
        column(x, True, 0 <= x < CELLS)

    @pl.loop(1, CELLS - 1)
    def _(x):
        column(x, False, True)

    @pl.loop(0, 20, unroll=4)
    def _(j):
        at = pl.ds(lax.rem(j + 22, FRAME), 1)
        for axis in range(3):
            value = vel[axis, j]
            before = jnp.where(row == 0, strip[0, 0, axis, at, :], spin(value, 1, 0))
            after = jnp.where(row == CELLS - 1, strip[1, 0, axis, at, :], spin(value, -1, 0))
            tall[axis, j] = 0.5 * value + 0.25 * (before + after)

    @pl.loop(0, 18, unroll=3)
    def _(j):
        for axis in range(3):
            value = 0.5 * tall[axis, j + 1] + 0.25 * (tall[axis, j] + tall[axis, j + 2])
            high, low = split(value)
            smooth[axis, j, :, :DEPTH] = high
            smooth[axis, j, :, DEPTH:] = low

    place = lax.broadcasted_iota(jnp.int32, (FRAME, DEPTH), 0)
    inside = (place <= CELLS) | (place == FRAME - 1)
    rim = [[], []]
    for s in range(2):
        for axis in range(3):
            value = 0.5 * strip[s, 0, axis] + 0.25 * (strip[s, 1, axis] + lines[s, axis])
            value = 0.5 * value + 0.25 * (spin(value, 1, 0) + spin(value, -1, 0))
            rim[s].append(jnp.where(inside, value, 0.0))

    goal = jnp.concatenate(split(table[...].T), axis=1)
    step = 256

    def hot(position, count):
        shape = (count, position.shape[1])
        return lax.broadcasted_iota(jnp.int32, shape, 0).astype(f32) == position

    def ones(mask):
        return jnp.where(mask, 1.0, 0.0).astype(bf16)

    def force_of(sources, count, spot, z, riser):
        at_z = ones(hot(z, DEPTH))
        picked = jnp.dot(
            sources, jnp.concatenate([at_z, at_z], axis=0), preferred_element_type=f32
        )
        at_riser = hot(riser, RISERS)
        weight = hot(spot, count)
        out = []
        for axis in range(3):
            start = 2 * RISERS + axis * count
            speed = picked[start : start + count]
            value = -jnp.sum(jnp.where(weight, speed, 0.0), axis=0, keepdims=True)
            if axis < 2:
                some = picked[axis * RISERS : (axis + 1) * RISERS]
                value = value + jnp.sum(jnp.where(at_riser, some, 0.0), axis=0, keepdims=True)
            out.append(2.0 * value)
        return at_z, out

    contract = (((1,), (1,)), ((), ()))

    def parts(force):
        found = []
        for value in force:
            high, low = split(value)
            found.append((high.astype(f32), low.astype(f32)))
        return found

    def spread(count, spot, at_z, force):
        weight = hot(spot, count)
        halves = []
        for half in range(2):
            rows = [jnp.where(weight, value[half], 0.0) for value in parts(force)]
            halves.append(jnp.concatenate(rows, axis=0).astype(bf16))
        return lax.dot_general(
            jnp.concatenate(halves, axis=1),
            jnp.concatenate([at_z, at_z], axis=1),
            contract,
            preferred_element_type=f32,
        )

    def take(slab, attr, n):
        at = attr * 4 + 2 * n
        return jnp.concatenate([slab[at : at + 1, :], slab[at + 1 : at + 2, :]], axis=1)

    inner = [smooth[axis, 1 : CELLS + 1].reshape(CELLS * CELLS, 2 * DEPTH) for axis in range(3)]
    sources = jnp.concatenate([goal, *inner], axis=0)
    total = None
    for n in range(MARKS // step):
        here = slice(n * step, (n + 1) * step)
        mx, my, mz, riser = (
            m[:, here].astype(f32) for m in (own_x, own_y, own_z, own_riser)
        )
        spot = mx * CELLS + my
        _, force = force_of(sources, CELLS * CELLS, spot, mz, riser)
        where_z = hot(mz, DEPTH)
        halves = []
        for half in range(2):
            rows = [jnp.where(where_z, value[half], 0.0) for value in parts(force)]
            halves.append(jnp.concatenate(rows, axis=0).astype(bf16))
        at_cell = ones(hot(spot, CELLS * CELLS))
        got = lax.dot_general(
            jnp.concatenate([at_cell, at_cell], axis=1),
            jnp.concatenate(halves, axis=1),
            contract,
            preferred_element_type=f32,
        )
        total = got if total is None else total + got
        for axis in range(3):
            push[axis, :, here] = force[axis]
    for axis in range(3):
        impulse[axis, 1 : CELLS + 1] = total[:, axis * DEPTH : (axis + 1) * DEPTH].reshape(
            CELLS, CELLS, DEPTH
        )
    for message, at, spot_x in ((xlow, CELLS - 1, 0), (xhigh, 0, CELLS + 1)):
        sources = jnp.concatenate([goal, *(smooth[axis, spot_x] for axis in range(3))], axis=0)
        slab = message[SLABS].astype(f32)
        total = None
        for n in range(MARKS // step):
            mx, my, mz, riser = (take(slab, attr, n) for attr in range(4))
            spot = jnp.where(mx == at, my, -1.0)
            at_z, force = force_of(sources, CELLS, spot, mz, riser)
            got = spread(CELLS, spot, at_z, force)
            total = got if total is None else total + got
        for axis in range(3):
            impulse[axis, spot_x] = total[axis * CELLS : (axis + 1) * CELLS]
    for s, (message, at) in enumerate(((ylow, CELLS - 1), (yhigh, 0))):
        halves = [jnp.concatenate(split(value), axis=1) for value in rim[s]]
        sources = jnp.concatenate([goal, *halves], axis=0)
        total = None
        for tile in range(3):
            slab = message[SLABS + tile].astype(f32)
            for n in range(MARKS // step):
                mx, my, mz, riser = (take(slab, attr, n) for attr in range(4))
                keep = my == at
                if tile == 1:
                    keep = keep & (mx == CELLS - 1)
                elif tile == 2:
                    keep = keep & (mx == 0)
                spot = jnp.where(keep, mx + (0, 8, CELLS)[tile], -1.0)
                at_z, force = force_of(sources, FRAME, spot, mz, riser)
                got = spread(FRAME, spot, at_z, force)
                total = got if total is None else total + got
        for axis in range(3):
            lines[s, axis] = total[axis * FRAME : (axis + 1) * FRAME]

    @pl.loop(0, 18, unroll=3)
    def _(j):
        at = pl.ds(lax.rem(j + 23, FRAME), 1)
        for axis in range(3):
            value = impulse[axis, j]
            before = jnp.where(row == 0, lines[0, axis, at, :], spin(value, 1, 0))
            after = jnp.where(row == CELLS - 1, lines[1, axis, at, :], spin(value, -1, 0))
            tall[axis, j] = 0.5 * value + 0.25 * (before + after)

    rate = 1.0 / RELAX
    gain = 1.0 - 0.5 / RELAX

    def collide(x):
        density = dens[0, x]
        own, speed = [], []
        for axis in range(3):
            value = 0.5 * tall[axis, x + 1] + 0.25 * (tall[axis, x] + tall[axis, x + 2])
            field[axis, x] = value
            own.append(value)
            speed.append((dens[1 + axis, x] + 0.5 * value) / density)
        square = speed[0] * speed[0] + speed[1] * speed[1] + speed[2] * speed[2]
        work = speed[0] * own[0] + speed[1] * own[1] + speed[2] * own[2]
        base = rate * density * (1.0 - 1.5 * square) - 3.0 * gain * work
        flow = [density * value for value in speed]
        even = [4.5 * rate * a + 9.0 * gain * b for a, b in zip(flow, own)]
        odd = [3.0 * rate * a + 3.0 * gain * b for a, b in zip(flow, own)]
        at = pl.ds(pl.multiple_of(x * CELLS, CELLS), CELLS)
        nxt[0, at, :] = (1.0 - rate) * nxt[0, at, :] + WEIGHT[0] * base
        for weight, indices in ((WEIGHT[1], (1, 3, 5)), (WEIGHT[7], (7, 9, 11, 13, 15, 17))):
            scaled = weight * base
            wide_even = [weight * value for value in even]
            wide_odd = [weight * value for value in odd]
            for index in indices:
                direction = VELOCITY[index]
                both = scaled + along(speed, direction) * along(wide_even, direction)
                apart = along(wide_odd, direction)
                nxt[index, at, :] = (1.0 - rate) * nxt[index, at, :] + (both + apart)
                nxt[index + 1, at, :] = (1.0 - rate) * nxt[index + 1, at, :] + (both - apart)

    copies = []
    chunk = 4
    for n in range(CELLS // chunk):

        @pl.loop(n * chunk, (n + 1) * chunk)
        def _(x):
            collide(x)

        cells_at = pl.ds(n * chunk * CELLS, chunk * CELLS)
        copies.append(
            pltpu.make_async_copy(nxt.at[:, cells_at, :], nxt_far.at[:, cells_at, :], sems.at[2 * n])
        )
        at = pl.ds(n * chunk, chunk)
        copies.append(pltpu.make_async_copy(field.at[:, at], field_far.at[:, at], sems.at[2 * n + 1]))
        for copy in copies[-2:]:
            copy.start()
    for copy in copies:
        copy.wait()


def on_device(populations, panels, modal_vel, marker_x, marker_y, marker_z, marker_riser):
    f32, bf16 = jnp.float32, jnp.bfloat16
    shape = jax.ShapeDtypeStruct
    devices = lax.axis_size("gx") * lax.axis_size("gy")
    cells = populations.reshape(19, CELLS * CELLS, DEPTH)
    marks = [m.reshape(1, MARKS) for m in (marker_x, marker_y, marker_z, marker_riser)]
    panel = panels.reshape(RISERS, -1)
    modes = panel.shape[1]
    vmem = pl.BlockSpec(memory_space=pltpu.VMEM)
    face = shape((SLABS + 1, CELLS, DEPTH), bf16)
    strip = shape((SLABS + 3, FRAME, DEPTH), bf16)

    def limit(mib):
        return pltpu.CompilerParams(vmem_limit_bytes=mib << 20)

    anywhere = pl.BlockSpec(memory_space=pl.ANY)
    xup, xdown, rows = pl.pallas_call(
        pack_x,
        out_shape=(face, face, shape((devices, 128), f32)),
        in_specs=[anywhere] * 7,
        out_specs=(vmem,) * 3,
        scratch_shapes=[
            *[pltpu.VMEM((19, 3 * CELLS, DEPTH), f32)] * 2,
            *[pltpu.VMEM((1, MARKS), jnp.int32)] * 4,
            pltpu.VMEM(panel.shape, bf16),
            pltpu.VMEM(modal_vel.shape, bf16),
            pltpu.VMEM((16, DEPTH), f32),
            pltpu.VMEM((2 * RISERS, modes), f32),
            pltpu.SemaphoreType.DMA((8,)),
        ],
        name="pack_x",
    )(cells, *marks, panel, modal_vel)

    def ring(axis, toward):
        size = lax.axis_size(axis)
        return [(i, (i + toward) % size) for i in range(size)]

    xlow = lax.ppermute(xup, "gx", ring("gx", 1))
    xhigh = lax.ppermute(xdown, "gx", ring("gx", -1))
    table = lax.all_to_all(rows, ("gx", "gy"), 0, 0, tiled=True)
    yup, ydown = pl.pallas_call(
        pack_y,
        out_shape=(strip, strip),
        in_specs=[vmem] * 7,
        out_specs=(vmem,) * 2,
        scratch_shapes=[
            *[pltpu.VMEM((SLABS + 1, CELLS, DEPTH), f32)] * 2,
            pltpu.VMEM((16, DEPTH), f32),
        ],
        compiler_params=limit(8),
        name="pack_y",
    )(cells, xlow, xhigh, *marks)
    ylow = lax.ppermute(yup, "gy", ring("gy", 1))
    yhigh = lax.ppermute(ydown, "gy", ring("gy", -1))
    nxt, push, field = pl.pallas_call(
        step_kernel,
        out_shape=(
            shape((19, CELLS * CELLS, DEPTH), f32),
            shape((3, 1, MARKS), f32),
            shape((3, CELLS, CELLS, DEPTH), f32),
        ),
        in_specs=[vmem] * 10,
        out_specs=(anywhere, vmem, anywhere),
        scratch_shapes=[
            pltpu.VMEM((19, CELLS * CELLS, DEPTH), f32),
            pltpu.VMEM((3, CELLS, CELLS, DEPTH), f32),
            pltpu.VMEM((19, 8 * CELLS, DEPTH), f32),
            pltpu.VMEM((2, 5, FRAME, DEPTH), f32),
            pltpu.VMEM((2, 2, 3, FRAME, DEPTH), f32),
            pltpu.VMEM((2, 3, FRAME, DEPTH), f32),
            pltpu.VMEM((3, 20, CELLS, DEPTH), f32),
            pltpu.VMEM((3, 20, CELLS, DEPTH), f32),
            pltpu.VMEM((3, 18, CELLS, 2 * DEPTH), bf16),
            pltpu.VMEM((4, CELLS, CELLS, DEPTH), f32),
            pltpu.VMEM((3, 18, CELLS, DEPTH), f32),
            pltpu.SemaphoreType.DMA((8,)),
        ],
        compiler_params=limit(32),
        name="step_kernel",
    )(cells, xlow, xhigh, ylow, yhigh, *marks, table)
    return (
        nxt.reshape(19, CELLS, CELLS, DEPTH),
        push.transpose(1, 0, 2)[None],
        field,
    )


def solution(mesh):
    in_specs = (
        P(None, "gx", "gy", None),
        P(None, None, ("gx", "gy")),
        P(),
        P("gx", "gy", None),
        P("gx", "gy", None),
        P("gx", "gy", None),
        P("gx", "gy", None),
    )
    out_specs = (P(None, "gx", "gy", None), P("gx", "gy", None, None), P(None, "gx", "gy", None))
    return jax.shard_map(on_device, mesh=mesh, in_specs=in_specs, out_specs=out_specs, check_vma=False)
```

```python
import jax
import jax.numpy as jnp
from jax import lax
from jax.experimental import pallas as pl
from jax.experimental.pallas import tpu as pltpu
from jax.sharding import PartitionSpec as P

VELOCITY = (
    (0, 0, 0),
    (1, 0, 0),
    (-1, 0, 0),
    (0, 1, 0),
    (0, -1, 0),
    (0, 0, 1),
    (0, 0, -1),
    (1, 1, 0),
    (-1, -1, 0),
    (1, -1, 0),
    (-1, 1, 0),
    (1, 0, 1),
    (-1, 0, -1),
    (1, 0, -1),
    (-1, 0, 1),
    (0, 1, 1),
    (0, -1, -1),
    (0, 1, -1),
    (0, -1, 1),
)
WEIGHT = (1.0 / 3.0,) + (1.0 / 18.0,) * 6 + (1.0 / 36.0,) * 12
RELAX = 0.8
CELLS = 16
DEPTH = 128
MARKS = 512
RISERS = 64
FRAME = 24


def slabs(axis, toward):
    order = []
    for layer in (1, 2, 3):
        for index in range(19):
            if VELOCITY[index][axis] * toward >= layer - 2:
                order.append((layer, index))
    return order


ORDER = {(axis, toward): slabs(axis, toward) for axis in (0, 1) for toward in (1, -1)}
PLACE = {key: {slab: k for k, slab in enumerate(order)} for key, order in ORDER.items()}
SLABS = len(ORDER[0, 1])
INTO = 5
SUMS = 7
YSLABS = INTO + 2 * SUMS
INWARD = {toward: [i for i in range(19) if VELOCITY[i][1] == toward] for toward in (1, -1)}


def near(layer, toward):
    return CELLS - layer if toward == 1 else layer - 1


def encode(value, index):
    return (value - WEIGHT[index]).astype(jnp.bfloat16)


def decode(value, index):
    return value.astype(jnp.float32) + WEIGHT[index]


def split(value):
    high = value.astype(jnp.bfloat16)
    low = (value - high.astype(jnp.float32)).astype(jnp.bfloat16)
    return high, low


def pack_x(
    cells_far, mx_far, my_far, mz_far, riser_far, panel_far, modal_far,
    xup, xdown, rows,
    first, last, mx, my, mz, riser, panel, modal, marks, pairs, sems,
):
    span = 3 * CELLS
    copies = [
        pltpu.make_async_copy(far, here, sems.at[n])
        for n, (far, here) in enumerate(
            (
                (modal_far, modal),
                (panel_far, panel),
                (mx_far, mx),
                (my_far, my),
                (mz_far, mz),
                (riser_far, riser),
                (cells_far.at[:, pl.ds(0, span), :], first),
                (cells_far.at[:, pl.ds(CELLS * CELLS - span, span), :], last),
            )
        )
    ]
    for copy in copies:
        copy.start()
    for copy in copies[:6]:
        copy.wait()
    fill_marks(marks, (mx, my, mz, riser))
    for n in range(RISERS):
        both = modal[n].astype(jnp.float32)
        for d in range(2):
            pairs[d * RISERS + n : d * RISERS + n + 1, :] = both[d : d + 1]
    product = lax.dot_general(
        panel[...],
        pairs[...].astype(jnp.bfloat16),
        (((1,), (1,)), ((), ())),
        preferred_element_type=jnp.float32,
    )
    mine = lax.broadcasted_iota(jnp.int32, product.shape, 0) == (
        lax.broadcasted_iota(jnp.int32, product.shape, 1) & (RISERS - 1)
    )
    row = jnp.sum(jnp.where(mine, product, 0.0), axis=0, keepdims=True)
    rows[...] = jnp.broadcast_to(row, rows.shape)
    for copy in copies[6:]:
        copy.wait()
    for out, toward in ((xup, 1), (xdown, -1)):
        for k, (layer, index) in enumerate(ORDER[0, toward]):
            if toward == 1:
                value = last[index, (3 - layer) * CELLS : (4 - layer) * CELLS, :]
            else:
                value = first[index, (layer - 1) * CELLS : layer * CELLS, :]
            out[k] = encode(value, index)
        out[SLABS] = marks[...].astype(jnp.bfloat16)


def fill_marks(marks, sources):
    for attr, source in enumerate(sources):
        for n in range(4):
            marks[attr * 4 + n : attr * 4 + n + 1, :] = source[:, n * 128 : (n + 1) * 128].astype(
                jnp.float32
            )


def pack_y(cells, xlow, xhigh, mx, my, mz, riser, yup, ydown, low, high, marks):
    low[...] = xlow[...].astype(jnp.float32)
    high[...] = xhigh[...].astype(jnp.float32)
    fill_marks(marks, (mx, my, mz, riser))
    place = lax.broadcasted_iota(jnp.int32, (8, DEPTH), 0)
    none = jnp.zeros((8, DEPTH), jnp.float32)

    def frame(layer, index, toward):
        row = near(layer, toward)
        tile = none
        for depth in (1, 2, 3):
            for source, side, at in ((high, -1, depth - 1), (low, 1, 8 - depth)):
                slot = PLACE[0, side].get((depth, index))
                if slot is not None:
                    tile = jnp.where(place == at, source[slot, row : row + 1, :], tile)
        own = cells[index, pl.ds(row, CELLS, stride=CELLS), :] - WEIGHT[index]
        return jnp.concatenate([own, tile], axis=0)

    for out, toward in ((yup, 1), (ydown, -1)):
        for n, index in enumerate(INWARD[toward]):
            out[n] = frame(1, index, toward).astype(jnp.bfloat16)

        def reads(cell):
            for index in range(19):
                cx, cy, cz = VELOCITY[index]
                layer = cell + toward * cy
                if layer:
                    value = frame(layer, index, toward) + WEIGHT[index]
                    yield index, spin(spin(value, cx, 0), cz, 1)

        density, momentum = moments(reads(2))
        sums = [value / density for value in momentum]
        density, momentum = moments(reads(1))
        for k, value in enumerate([*sums, density, *momentum]):
            out[INTO + 2 * k], out[INTO + 2 * k + 1] = split(value)
        for n, source in enumerate((marks[...], low[SLABS], high[SLABS])):
            out[YSLABS + n] = jnp.concatenate([source, none], axis=0).astype(jnp.bfloat16)


def moments(reads):
    density = None
    momentum = [None, None, None]
    for index, value in reads:
        density = value if density is None else density + value
        for axis in range(3):
            sign = VELOCITY[index][axis]
            if sign == 1:
                momentum[axis] = value if momentum[axis] is None else momentum[axis] + value
            elif sign == -1:
                momentum[axis] = -value if momentum[axis] is None else momentum[axis] - value
    return density, momentum


def along(vector, direction):
    total = None
    for axis in range(3):
        if direction[axis] == 1:
            total = vector[axis] if total is None else total + vector[axis]
        elif direction[axis] == -1:
            total = -vector[axis] if total is None else total - vector[axis]
    return total


def spin(value, shift, axis):
    return pltpu.roll(value, shift % value.shape[axis], axis) if shift else value


def columns(cells, xlow, xhigh, sums, vel, smooth, share, side, tall):
    def rows_of(column):
        return slice(column * CELLS, (column + 1) * CELLS)

    for message, toward in ((xlow, 1), (xhigh, -1)):
        for k, (layer, index) in enumerate(ORDER[0, toward]):
            column = 8 - layer if toward == 1 else layer - 1
            side[index, rows_of(column), :] = decode(message[k], index)

    for s, toward in enumerate((1, -1)):
        first = 0 if toward == 1 else CELLS - 1

        def outward():
            for index in INWARD[-toward]:
                cx, _, cz = VELOCITY[index]
                value = jnp.concatenate(
                    [
                        cells[index, pl.ds(first, CELLS, stride=CELLS), :],
                        side[index, pl.ds(first, 8, stride=CELLS), :],
                    ],
                    axis=0,
                )
                yield index, spin(spin(value, cx, 0), cz, 1)

        density, momentum = moments(outward())
        for k, value in enumerate([density, *momentum]):
            share[s, k] = value

    row = lax.broadcasted_iota(jnp.int32, (CELLS, DEPTH), 0)

    def one(x, known):
        if known:
            here = rows_of(x % FRAME)
        else:
            here = pl.ds(pl.multiple_of(x * CELLS, CELLS), CELLS)

        def reads():
            for index in range(19):
                cx, cy, cz = VELOCITY[index]
                if known:
                    at = (x - cx) % FRAME
                    if at < CELLS:
                        value = cells[index, rows_of(at), :]
                    else:
                        value = side[index, rows_of(at - CELLS), :]
                else:
                    at = x - cx
                    value = cells[index, pl.ds(pl.multiple_of(at * CELLS, CELLS), CELLS), :]
                if cy:
                    value = jnp.where(row == (0 if cy == 1 else CELLS - 1), 0.0, spin(value, cy, 0))
                value = spin(value, cz, 1)
                yield index, value

        density, momentum = moments(reads())
        sums[0, here, :] = density
        for axis in range(3):
            sums[1 + axis, here, :] = momentum[axis]
            vel[axis, here, :] = momentum[axis] / density

    for x in (-2, -1, 0, CELLS - 1, CELLS, CELLS + 1):
        one(x, True)

    @pl.loop(1, CELLS - 1)
    def _(x):
        one(x, False)

    def start(x):
        return pl.ds(pl.multiple_of(lax.rem(x + FRAME, FRAME) * CELLS, CELLS), CELLS)

    @pl.loop(0, 20, unroll=4)
    def _(j):
        for axis in range(3):
            value = vel[axis, start(j - 2), :]
            tall[axis, j] = 0.5 * value + 0.25 * (spin(value, 1, 0) + spin(value, -1, 0))

    @pl.loop(0, 18, unroll=3)
    def _(j):
        for axis in range(3):
            smooth[axis, start(j - 1), :] = 0.5 * tall[axis, j + 1] + 0.25 * (
                tall[axis, j] + tall[axis, j + 2]
            )


def step_kernel(
    cells_far, sums, vel, almost, share, xlow, xhigh, ylow, yhigh, own_x, own_y, own_z, own_riser, table,
    nxt_far, push, field_far,
    wide, nxt, field, edge, lines, tall, smooth, dens, impulse, sems,
):
    f32, bf16 = jnp.float32, jnp.bfloat16
    rate = 1.0 / RELAX
    gain = 1.0 - 0.5 / RELAX
    row = lax.broadcasted_iota(jnp.int32, (CELLS, DEPTH), 0)
    place = lax.broadcasted_iota(jnp.int32, (FRAME, DEPTH), 0)
    inside = (place <= CELLS) | (place == FRAME - 1)
    last = (FRAME - 1) * CELLS
    fetch = pltpu.make_async_copy(
        cells_far, wide.at[:, pl.ds(CELLS, CELLS * CELLS), :], sems.at[8]
    )
    fetch.start()
    for message, toward in ((xlow, 1), (xhigh, -1)):
        column = 0 if toward == 1 else CELLS + 1
        for index in range(19):
            if VELOCITY[index][0] == toward:
                here = slice(column * CELLS, (column + 1) * CELLS)
                wide[index, here, :] = decode(message[PLACE[0, toward][1, index]], index)
    dens[...] = sums[:, : CELLS * CELLS, :]
    smooth[:, : (CELLS + 1) * CELLS, :] = almost[:, : (CELLS + 1) * CELLS, :]
    smooth[:, last:, :] = almost[:, last:, :]

    def over_x(value):
        return 0.5 * value + 0.25 * (spin(value, 1, 0) + spin(value, -1, 0))

    rim = [[], []]
    for s, (toward, message) in enumerate(((1, ylow), (-1, yhigh))):
        first = 0 if toward == 1 else CELLS - 1

        def crossing():
            for n, index in enumerate(INWARD[toward]):
                cx, _, cz = VELOCITY[index]
                value = spin(spin(decode(message[n], index), cx, 0), cz, 1)
                edge[s, n] = value
                yield index, value

        density, momentum = moments(crossing())
        whole = []
        for k, value in enumerate([density, *momentum]):
            value = value + sums[k, pl.ds(first, FRAME, stride=CELLS), :]
            dens[k, pl.ds(first, CELLS, stride=CELLS), :] = value[:CELLS]
            whole.append(value)
        sent = [
            message[INTO + 2 * k].astype(f32) + message[INTO + 2 * k + 1].astype(f32)
            for k in range(SUMS)
        ]
        outer = [sent[3 + k] + share[s, k] for k in range(4)]
        for axis in range(3):
            beyond = outer[1 + axis] / outer[0]
            at_edge = whole[1 + axis] / whole[0]
            second = pl.ds(first + toward, FRAME, stride=CELLS)
            third = pl.ds(first + 2 * toward, FRAME, stride=CELLS)
            inner = vel[axis, second, :]
            smooth[axis, pl.ds(first, FRAME, stride=CELLS), :] = over_x(
                0.5 * at_edge + 0.25 * (beyond + inner)
            )
            smooth[axis, second, :] = over_x(0.5 * inner + 0.25 * (at_edge + vel[axis, third, :]))
            value = over_x(0.5 * beyond + 0.25 * (sent[axis] + at_edge))
            rim[s].append(jnp.where(inside, value, 0.0))

    goal = jnp.concatenate(split(table[...].T), axis=1)
    step = 256

    def hot(position, count):
        shape = (count, position.shape[1])
        return lax.broadcasted_iota(jnp.int32, shape, 0).astype(f32) == position

    def ones(mask):
        return jnp.where(mask, 1.0, 0.0).astype(bf16)

    def force_of(sources, count, spot, z, riser):
        at_z = ones(hot(z, DEPTH))
        picked = jnp.dot(
            sources, jnp.concatenate([at_z, at_z], axis=0), preferred_element_type=f32
        )
        at_riser = hot(riser, RISERS)
        weight = hot(spot, count)
        out = []
        for axis in range(3):
            start = 2 * RISERS + axis * count
            speed = picked[start : start + count]
            value = -jnp.sum(jnp.where(weight, speed, 0.0), axis=0, keepdims=True)
            if axis < 2:
                some = picked[axis * RISERS : (axis + 1) * RISERS]
                value = value + jnp.sum(jnp.where(at_riser, some, 0.0), axis=0, keepdims=True)
            out.append(2.0 * value)
        return at_z, out

    contract = (((1,), (1,)), ((), ()))

    def parts(force):
        found = []
        for value in force:
            high, low = split(value)
            found.append((high.astype(f32), low.astype(f32)))
        return found

    def spread(count, spot, at_z, force):
        weight = hot(spot, count)
        halves = []
        for half in range(2):
            rows = [jnp.where(weight, value[half], 0.0) for value in parts(force)]
            halves.append(jnp.concatenate(rows, axis=0).astype(bf16))
        return lax.dot_general(
            jnp.concatenate(halves, axis=1),
            jnp.concatenate([at_z, at_z], axis=1),
            contract,
            preferred_element_type=f32,
        )

    def take(slab, attr, n):
        at = attr * 4 + 2 * n
        return jnp.concatenate([slab[at : at + 1, :], slab[at + 1 : at + 2, :]], axis=1)

    def halves_of(axis, column, count):
        value = smooth[axis, column * CELLS : (column + count) * CELLS, :]
        return jnp.concatenate(split(value), axis=1)

    sources = jnp.concatenate([goal, *(halves_of(axis, 0, CELLS) for axis in range(3))], axis=0)
    total = None
    for n in range(MARKS // step):
        here = slice(n * step, (n + 1) * step)
        mx, my, mz, riser = (
            m[:, here].astype(f32) for m in (own_x, own_y, own_z, own_riser)
        )
        spot = mx * CELLS + my
        _, force = force_of(sources, CELLS * CELLS, spot, mz, riser)
        where_z = hot(mz, DEPTH)
        halves = []
        for half in range(2):
            rows = [jnp.where(where_z, value[half], 0.0) for value in parts(force)]
            halves.append(jnp.concatenate(rows, axis=0).astype(bf16))
        at_cell = ones(hot(spot, CELLS * CELLS))
        got = lax.dot_general(
            jnp.concatenate([at_cell, at_cell], axis=1),
            jnp.concatenate(halves, axis=1),
            contract,
            preferred_element_type=f32,
        )
        total = got if total is None else total + got
        for axis in range(3):
            push[axis, :, here] = force[axis]
    for axis in range(3):
        impulse[axis, 1 : CELLS + 1] = total[:, axis * DEPTH : (axis + 1) * DEPTH].reshape(
            CELLS, CELLS, DEPTH
        )
    for message, at, spot_x in ((xlow, CELLS - 1, 0), (xhigh, 0, CELLS + 1)):
        column = (spot_x - 1) % FRAME
        sources = jnp.concatenate([goal, *(halves_of(axis, column, 1) for axis in range(3))], axis=0)
        slab = message[SLABS].astype(f32)
        total = None
        for n in range(MARKS // step):
            mx, my, mz, riser = (take(slab, attr, n) for attr in range(4))
            spot = jnp.where(mx == at, my, -1.0)
            at_z, force = force_of(sources, CELLS, spot, mz, riser)
            got = spread(CELLS, spot, at_z, force)
            total = got if total is None else total + got
        for axis in range(3):
            impulse[axis, spot_x] = total[axis * CELLS : (axis + 1) * CELLS]
    for s, (message, at) in enumerate(((ylow, CELLS - 1), (yhigh, 0))):
        halves = [jnp.concatenate(split(value), axis=1) for value in rim[s]]
        sources = jnp.concatenate([goal, *halves], axis=0)
        total = None
        for tile in range(3):
            slab = message[YSLABS + tile].astype(f32)
            for n in range(MARKS // step):
                mx, my, mz, riser = (take(slab, attr, n) for attr in range(4))
                keep = my == at
                if tile == 1:
                    keep = keep & (mx == CELLS - 1)
                elif tile == 2:
                    keep = keep & (mx == 0)
                spot = jnp.where(keep, mx + (0, 8, CELLS)[tile], -1.0)
                at_z, force = force_of(sources, FRAME, spot, mz, riser)
                got = spread(FRAME, spot, at_z, force)
                total = got if total is None else total + got
        for axis in range(3):
            lines[s, axis] = total[axis * FRAME : (axis + 1) * FRAME]

    @pl.loop(0, 18, unroll=3)
    def _(j):
        at = pl.ds(lax.rem(j + 23, FRAME), 1)
        for axis in range(3):
            value = impulse[axis, j]
            before = jnp.where(row == 0, lines[0, axis, at, :], spin(value, 1, 0))
            after = jnp.where(row == CELLS - 1, lines[1, axis, at, :], spin(value, -1, 0))
            tall[axis, j] = 0.5 * value + 0.25 * (before + after)

    def streamed(x, index):
        cx, cy, cz = VELOCITY[index]
        start = pl.multiple_of((x + (1 - cx)) * CELLS, CELLS)
        value = spin(spin(wide[index, pl.ds(start, CELLS), :], cy, 0), cz, 1)
        if cy:
            line = edge[0 if cy == 1 else 1, INWARD[cy].index(index), pl.ds(x, 1), :]
            value = jnp.where(row == (0 if cy == 1 else CELLS - 1), line, value)
        return (1.0 - rate) * value

    def collide(x):
        at = pl.ds(pl.multiple_of(x * CELLS, CELLS), CELLS)
        density = dens[0, at, :]
        own, speed = [], []
        for axis in range(3):
            value = 0.5 * tall[axis, x + 1] + 0.25 * (tall[axis, x] + tall[axis, x + 2])
            field[axis, x] = value
            own.append(value)
            speed.append((dens[1 + axis, at, :] + 0.5 * value) / density)
        square = speed[0] * speed[0] + speed[1] * speed[1] + speed[2] * speed[2]
        work = speed[0] * own[0] + speed[1] * own[1] + speed[2] * own[2]
        base = rate * density * (1.0 - 1.5 * square) - 3.0 * gain * work
        flow = [density * value for value in speed]
        even = [4.5 * rate * a + 9.0 * gain * b for a, b in zip(flow, own)]
        odd = [3.0 * rate * a + 3.0 * gain * b for a, b in zip(flow, own)]
        nxt[0, at, :] = streamed(x, 0) + WEIGHT[0] * base
        for weight, indices in ((WEIGHT[1], (1, 3, 5)), (WEIGHT[7], (7, 9, 11, 13, 15, 17))):
            scaled = weight * base
            wide_even = [weight * value for value in even]
            wide_odd = [weight * value for value in odd]
            for index in indices:
                direction = VELOCITY[index]
                both = scaled + along(speed, direction) * along(wide_even, direction)
                apart = along(wide_odd, direction)
                nxt[index, at, :] = streamed(x, index) + (both + apart)
                nxt[index + 1, at, :] = streamed(x, index + 1) + (both - apart)

    fetch.wait()
    copies = []
    chunk = 4
    for n in range(CELLS // chunk):

        @pl.loop(n * chunk, (n + 1) * chunk, unroll=2)
        def _(x):
            collide(x)

        cells_at = pl.ds(n * chunk * CELLS, chunk * CELLS)
        copies.append(
            pltpu.make_async_copy(nxt.at[:, cells_at, :], nxt_far.at[:, cells_at, :], sems.at[2 * n])
        )
        at = pl.ds(n * chunk, chunk)
        copies.append(pltpu.make_async_copy(field.at[:, at], field_far.at[:, at], sems.at[2 * n + 1]))
        for copy in copies[-2:]:
            copy.start()
    for copy in copies:
        copy.wait()


def on_device(populations, panels, modal_vel, marker_x, marker_y, marker_z, marker_riser):
    f32, bf16 = jnp.float32, jnp.bfloat16
    shape = jax.ShapeDtypeStruct
    devices = lax.axis_size("gx") * lax.axis_size("gy")
    cells = populations.reshape(19, CELLS * CELLS, DEPTH)
    marks = [m.reshape(1, MARKS) for m in (marker_x, marker_y, marker_z, marker_riser)]
    panel = panels.reshape(RISERS, -1)
    modes = panel.shape[1]
    vmem = pl.BlockSpec(memory_space=pltpu.VMEM)
    face = shape((SLABS + 1, CELLS, DEPTH), bf16)
    strip = shape((YSLABS + 3, FRAME, DEPTH), bf16)

    def limit(mib):
        return pltpu.CompilerParams(vmem_limit_bytes=mib << 20)

    anywhere = pl.BlockSpec(memory_space=pl.ANY)
    xup, xdown, rows = pl.pallas_call(
        pack_x,
        out_shape=(face, face, shape((devices, 128), f32)),
        in_specs=[anywhere] * 7,
        out_specs=(vmem,) * 3,
        scratch_shapes=[
            *[pltpu.VMEM((19, 3 * CELLS, DEPTH), f32)] * 2,
            *[pltpu.VMEM((1, MARKS), jnp.int32)] * 4,
            pltpu.VMEM(panel.shape, bf16),
            pltpu.VMEM(modal_vel.shape, bf16),
            pltpu.VMEM((16, DEPTH), f32),
            pltpu.VMEM((2 * RISERS, modes), f32),
            pltpu.SemaphoreType.DMA((8,)),
        ],
        name="pack_x",
    )(cells, *marks, panel, modal_vel)

    def ring(axis, toward):
        size = lax.axis_size(axis)
        return [(i, (i + toward) % size) for i in range(size)]

    xlow = lax.ppermute(xup, "gx", ring("gx", 1))
    xhigh = lax.ppermute(xdown, "gx", ring("gx", -1))
    table = lax.all_to_all(rows, ("gx", "gy"), 0, 0, tiled=True)
    yup, ydown = pl.pallas_call(
        pack_y,
        out_shape=(strip, strip),
        in_specs=[vmem] * 7,
        out_specs=(vmem,) * 2,
        scratch_shapes=[
            *[pltpu.VMEM((SLABS + 1, CELLS, DEPTH), f32)] * 2,
            pltpu.VMEM((16, DEPTH), f32),
        ],
        compiler_params=limit(8),
        name="pack_y",
    )(cells, xlow, xhigh, *marks)
    ylow = lax.ppermute(yup, "gy", ring("gy", 1))
    yhigh = lax.ppermute(ydown, "gy", ring("gy", -1))
    early = pl.pallas_call(
        columns,
        out_shape=(
            shape((4, FRAME * CELLS, DEPTH), f32),
            shape((3, FRAME * CELLS, DEPTH), f32),
            shape((3, FRAME * CELLS, DEPTH), f32),
            shape((2, 4, FRAME, DEPTH), f32),
        ),
        in_specs=[vmem] * 3,
        out_specs=(vmem,) * 4,
        scratch_shapes=[
            pltpu.VMEM((19, 8 * CELLS, DEPTH), f32),
            pltpu.VMEM((3, 20, CELLS, DEPTH), f32),
        ],
        compiler_params=limit(12),
        name="columns",
    )(cells, xlow, xhigh)
    nxt, push, field = pl.pallas_call(
        step_kernel,
        out_shape=(
            shape((19, CELLS * CELLS, DEPTH), f32),
            shape((3, 1, MARKS), f32),
            shape((3, CELLS, CELLS, DEPTH), f32),
        ),
        in_specs=[anywhere] + [vmem] * 13,
        out_specs=(anywhere, vmem, anywhere),
        scratch_shapes=[
            pltpu.VMEM((19, (CELLS + 2) * CELLS, DEPTH), f32),
            pltpu.VMEM((19, CELLS * CELLS, DEPTH), f32),
            pltpu.VMEM((3, CELLS, CELLS, DEPTH), f32),
            pltpu.VMEM((2, INTO, FRAME, DEPTH), f32),
            pltpu.VMEM((2, 3, FRAME, DEPTH), f32),
            pltpu.VMEM((3, 18, CELLS, DEPTH), f32),
            pltpu.VMEM((3, FRAME * CELLS, DEPTH), f32),
            pltpu.VMEM((4, CELLS * CELLS, DEPTH), f32),
            pltpu.VMEM((3, 18, CELLS, DEPTH), f32),
            pltpu.SemaphoreType.DMA((9,)),
        ],
        compiler_params=limit(60),
        name="step_kernel",
    )(cells, *early, xlow, xhigh, ylow, yhigh, *marks, table)
    return (
        nxt.reshape(19, CELLS, CELLS, DEPTH),
        push.transpose(1, 0, 2)[None],
        field,
    )


def solution(mesh):
    in_specs = (
        P(None, "gx", "gy", None),
        P(None, None, ("gx", "gy")),
        P(),
        P("gx", "gy", None),
        P("gx", "gy", None),
        P("gx", "gy", None),
        P("gx", "gy", None),
    )
    out_specs = (P(None, "gx", "gy", None), P("gx", "gy", None, None), P(None, "gx", "gy", None))
    return jax.shard_map(on_device, mesh=mesh, in_specs=in_specs, out_specs=out_specs, check_vma=False)
```

```python
import jax
import jax.numpy as jnp
from jax import lax
from jax.experimental import pallas as pl
from jax.experimental.pallas import tpu as pltpu
from jax.sharding import PartitionSpec as P

VELOCITY = (
    (0, 0, 0),
    (1, 0, 0),
    (-1, 0, 0),
    (0, 1, 0),
    (0, -1, 0),
    (0, 0, 1),
    (0, 0, -1),
    (1, 1, 0),
    (-1, -1, 0),
    (1, -1, 0),
    (-1, 1, 0),
    (1, 0, 1),
    (-1, 0, -1),
    (1, 0, -1),
    (-1, 0, 1),
    (0, 1, 1),
    (0, -1, -1),
    (0, 1, -1),
    (0, -1, 1),
)
WEIGHT = (1.0 / 3.0,) + (1.0 / 18.0,) * 6 + (1.0 / 36.0,) * 12
RELAX = 0.8
CELLS = 16
DEPTH = 128
MARKS = 512
RISERS = 64
FRAME = 24


def slabs(axis, toward):
    order = []
    for layer in (1, 2, 3):
        for index in range(19):
            if VELOCITY[index][axis] * toward >= layer - 2:
                order.append((layer, index))
    return order


ORDER = {(axis, toward): slabs(axis, toward) for axis in (0, 1) for toward in (1, -1)}
PLACE = {key: {slab: k for k, slab in enumerate(order)} for key, order in ORDER.items()}
SLABS = len(ORDER[0, 1])
INTO = 5
SUMS = 7
YSLABS = INTO + 2 * SUMS
INWARD = {toward: [i for i in range(19) if VELOCITY[i][1] == toward] for toward in (1, -1)}


def near(layer, toward):
    return CELLS - layer if toward == 1 else layer - 1


def encode(value, index):
    return (value - WEIGHT[index]).astype(jnp.bfloat16)


def decode(value, index):
    return value.astype(jnp.float32) + WEIGHT[index]


def split(value):
    high = value.astype(jnp.bfloat16)
    low = (value - high.astype(jnp.float32)).astype(jnp.bfloat16)
    return high, low


def pack_x(
    cells_far, mx_far, my_far, mz_far, riser_far, panel_far, modal_far,
    xup, xdown, rows,
    first, last, mx, my, mz, riser, panel, modal, marks, pairs, sems,
):
    span = 3 * CELLS
    copies = [
        pltpu.make_async_copy(far, here, sems.at[n])
        for n, (far, here) in enumerate(
            (
                (modal_far, modal),
                (panel_far, panel),
                (mx_far, mx),
                (my_far, my),
                (mz_far, mz),
                (riser_far, riser),
                (cells_far.at[:, pl.ds(0, span), :], first),
                (cells_far.at[:, pl.ds(CELLS * CELLS - span, span), :], last),
            )
        )
    ]
    for copy in copies:
        copy.start()
    for copy in copies[:6]:
        copy.wait()
    fill_marks(marks, (mx, my, mz, riser))
    for n in range(RISERS):
        both = modal[n].astype(jnp.float32)
        for d in range(2):
            pairs[d * RISERS + n : d * RISERS + n + 1, :] = both[d : d + 1]
    product = lax.dot_general(
        panel[...],
        pairs[...].astype(jnp.bfloat16),
        (((1,), (1,)), ((), ())),
        preferred_element_type=jnp.float32,
    )
    mine = lax.broadcasted_iota(jnp.int32, product.shape, 0) == (
        lax.broadcasted_iota(jnp.int32, product.shape, 1) & (RISERS - 1)
    )
    row = jnp.sum(jnp.where(mine, product, 0.0), axis=0, keepdims=True)
    rows[...] = jnp.broadcast_to(row, rows.shape)
    for copy in copies[6:]:
        copy.wait()
    for out, toward in ((xup, 1), (xdown, -1)):
        for k, (layer, index) in enumerate(ORDER[0, toward]):
            if toward == 1:
                value = last[index, (3 - layer) * CELLS : (4 - layer) * CELLS, :]
            else:
                value = first[index, (layer - 1) * CELLS : layer * CELLS, :]
            out[k] = encode(value, index)
        out[SLABS] = marks[...].astype(jnp.bfloat16)


def fill_marks(marks, sources):
    for attr, source in enumerate(sources):
        for n in range(4):
            marks[attr * 4 + n : attr * 4 + n + 1, :] = source[:, n * 128 : (n + 1) * 128].astype(
                jnp.float32
            )


def pack_y(cells, xlow, xhigh, mx, my, mz, riser, yup, ydown, low, high, marks):
    low[...] = xlow[...].astype(jnp.float32)
    high[...] = xhigh[...].astype(jnp.float32)
    fill_marks(marks, (mx, my, mz, riser))
    place = lax.broadcasted_iota(jnp.int32, (8, DEPTH), 0)
    none = jnp.zeros((8, DEPTH), jnp.float32)

    def frame(layer, index, toward):
        row = near(layer, toward)
        tile = none
        for depth in (1, 2, 3):
            for source, side, at in ((high, -1, depth - 1), (low, 1, 8 - depth)):
                slot = PLACE[0, side].get((depth, index))
                if slot is not None:
                    tile = jnp.where(place == at, source[slot, row : row + 1, :], tile)
        own = cells[index, pl.ds(row, CELLS, stride=CELLS), :] - WEIGHT[index]
        return jnp.concatenate([own, tile], axis=0)

    for out, toward in ((yup, 1), (ydown, -1)):
        for n, index in enumerate(INWARD[toward]):
            out[n] = frame(1, index, toward).astype(jnp.bfloat16)

        def reads(cell):
            for index in range(19):
                cx, cy, cz = VELOCITY[index]
                layer = cell + toward * cy
                if layer:
                    value = frame(layer, index, toward) + WEIGHT[index]
                    yield index, spin(spin(value, cx, 0), cz, 1)

        density, momentum = moments(reads(2))
        sums = [value / density for value in momentum]
        density, momentum = moments(reads(1))
        for k, value in enumerate([*sums, density, *momentum]):
            out[INTO + 2 * k], out[INTO + 2 * k + 1] = split(value)
        for n, source in enumerate((marks[...], low[SLABS], high[SLABS])):
            out[YSLABS + n] = jnp.concatenate([source, none], axis=0).astype(jnp.bfloat16)


def moments(reads):
    density = None
    momentum = [None, None, None]
    for index, value in reads:
        density = value if density is None else density + value
        for axis in range(3):
            sign = VELOCITY[index][axis]
            if sign == 1:
                momentum[axis] = value if momentum[axis] is None else momentum[axis] + value
            elif sign == -1:
                momentum[axis] = -value if momentum[axis] is None else momentum[axis] - value
    return density, momentum


def along(vector, direction):
    total = None
    for axis in range(3):
        if direction[axis] == 1:
            total = vector[axis] if total is None else total + vector[axis]
        elif direction[axis] == -1:
            total = -vector[axis] if total is None else total - vector[axis]
    return total


def spin(value, shift, axis):
    return pltpu.roll(value, shift % value.shape[axis], axis) if shift else value


def views(state):
    return state.at[pl.ds(0, 4)], state.at[pl.ds(4, 3)], state.at[pl.ds(7, 3)]


def share_rows(side, k):
    return slice((4 * side + k) * FRAME, (4 * side + k + 1) * FRAME)


def columns(cells, xlow, xhigh, state, side, tall):
    sums, vel, smooth = views(state)

    def rows_of(column):
        return slice(column * CELLS, (column + 1) * CELLS)

    for message, toward in ((xlow, 1), (xhigh, -1)):
        for k, (layer, index) in enumerate(ORDER[0, toward]):
            column = 8 - layer if toward == 1 else layer - 1
            side[index, rows_of(column), :] = decode(message[k], index)

    for s, toward in enumerate((1, -1)):
        first = 0 if toward == 1 else CELLS - 1

        def outward():
            for index in INWARD[-toward]:
                cx, _, cz = VELOCITY[index]
                value = jnp.concatenate(
                    [
                        cells[index, pl.ds(first, CELLS, stride=CELLS), :],
                        side[index, pl.ds(first, 8, stride=CELLS), :],
                    ],
                    axis=0,
                )
                yield index, spin(spin(value, cx, 0), cz, 1)

        density, momentum = moments(outward())
        for k, value in enumerate([density, *momentum]):
            state[10, share_rows(s, k), :] = value

    row = lax.broadcasted_iota(jnp.int32, (CELLS, DEPTH), 0)

    def one(x, known):
        if known:
            here = rows_of(x % FRAME)
        else:
            here = pl.ds(pl.multiple_of(x * CELLS, CELLS), CELLS)

        def reads():
            for index in range(19):
                cx, cy, cz = VELOCITY[index]
                if known:
                    at = (x - cx) % FRAME
                    if at < CELLS:
                        value = cells[index, rows_of(at), :]
                    else:
                        value = side[index, rows_of(at - CELLS), :]
                else:
                    at = x - cx
                    value = cells[index, pl.ds(pl.multiple_of(at * CELLS, CELLS), CELLS), :]
                if cy:
                    value = jnp.where(row == (0 if cy == 1 else CELLS - 1), 0.0, spin(value, cy, 0))
                value = spin(value, cz, 1)
                yield index, value

        density, momentum = moments(reads())
        sums[0, here, :] = density
        for axis in range(3):
            sums[1 + axis, here, :] = momentum[axis]
            vel[axis, here, :] = momentum[axis] / density

    for x in (-2, -1, 0, CELLS - 1, CELLS, CELLS + 1):
        one(x, True)

    @pl.loop(1, CELLS - 1)
    def _(x):
        one(x, False)

    def start(x):
        return pl.ds(pl.multiple_of(lax.rem(x + FRAME, FRAME) * CELLS, CELLS), CELLS)

    @pl.loop(0, 20, unroll=4)
    def _(j):
        for axis in range(3):
            value = vel[axis, start(j - 2), :]
            tall[axis, j] = 0.5 * value + 0.25 * (spin(value, 1, 0) + spin(value, -1, 0))

    @pl.loop(0, 18, unroll=3)
    def _(j):
        for axis in range(3):
            smooth[axis, start(j - 1), :] = 0.5 * tall[axis, j + 1] + 0.25 * (
                tall[axis, j] + tall[axis, j + 2]
            )


def step_kernel(
    cells_far, state, xlow, xhigh, ylow, yhigh, own_x, own_y, own_z, own_riser, table,
    nxt_far, push, field_far,
    wide, nxt, field, edge, lines, tall, smooth, dens, impulse, sems,
):
    f32, bf16 = jnp.float32, jnp.bfloat16
    rate = 1.0 / RELAX
    gain = 1.0 - 0.5 / RELAX
    row = lax.broadcasted_iota(jnp.int32, (CELLS, DEPTH), 0)
    place = lax.broadcasted_iota(jnp.int32, (FRAME, DEPTH), 0)
    inside = (place <= CELLS) | (place == FRAME - 1)
    last = (FRAME - 1) * CELLS
    sums, vel, almost = views(state)
    fetch = pltpu.make_async_copy(
        cells_far, wide.at[:, pl.ds(CELLS, CELLS * CELLS), :], sems.at[8]
    )
    fetch.start()
    for message, toward in ((xlow, 1), (xhigh, -1)):
        column = 0 if toward == 1 else CELLS + 1
        for index in range(19):
            if VELOCITY[index][0] == toward:
                here = slice(column * CELLS, (column + 1) * CELLS)
                wide[index, here, :] = decode(message[PLACE[0, toward][1, index]], index)
    dens[...] = sums[:, : CELLS * CELLS, :]
    smooth[:, : (CELLS + 1) * CELLS, :] = almost[:, : (CELLS + 1) * CELLS, :]
    smooth[:, last:, :] = almost[:, last:, :]

    def over_x(value):
        return 0.5 * value + 0.25 * (spin(value, 1, 0) + spin(value, -1, 0))

    rim = [[], []]
    for s, (toward, message) in enumerate(((1, ylow), (-1, yhigh))):
        first = 0 if toward == 1 else CELLS - 1

        def crossing():
            for n, index in enumerate(INWARD[toward]):
                cx, _, cz = VELOCITY[index]
                value = spin(spin(decode(message[n], index), cx, 0), cz, 1)
                edge[s, n] = value
                yield index, value

        density, momentum = moments(crossing())
        whole = []
        for k, value in enumerate([density, *momentum]):
            value = value + sums[k, pl.ds(first, FRAME, stride=CELLS), :]
            dens[k, pl.ds(first, CELLS, stride=CELLS), :] = value[:CELLS]
            whole.append(value)
        sent = [
            message[INTO + 2 * k].astype(f32) + message[INTO + 2 * k + 1].astype(f32)
            for k in range(SUMS)
        ]
        outer = [sent[3 + k] + state[10, share_rows(s, k), :] for k in range(4)]
        for axis in range(3):
            beyond = outer[1 + axis] / outer[0]
            at_edge = whole[1 + axis] / whole[0]
            second = pl.ds(first + toward, FRAME, stride=CELLS)
            third = pl.ds(first + 2 * toward, FRAME, stride=CELLS)
            inner = vel[axis, second, :]
            smooth[axis, pl.ds(first, FRAME, stride=CELLS), :] = over_x(
                0.5 * at_edge + 0.25 * (beyond + inner)
            )
            smooth[axis, second, :] = over_x(0.5 * inner + 0.25 * (at_edge + vel[axis, third, :]))
            value = over_x(0.5 * beyond + 0.25 * (sent[axis] + at_edge))
            rim[s].append(jnp.where(inside, value, 0.0))

    goal = jnp.concatenate(split(table[...].T), axis=1)
    step = 256

    def hot(position, count):
        shape = (count, position.shape[1])
        return lax.broadcasted_iota(jnp.int32, shape, 0).astype(f32) == position

    def ones(mask):
        return jnp.where(mask, 1.0, 0.0).astype(bf16)

    def force_of(sources, count, spot, z, riser):
        at_z = ones(hot(z, DEPTH))
        picked = jnp.dot(
            sources, jnp.concatenate([at_z, at_z], axis=0), preferred_element_type=f32
        )
        at_riser = hot(riser, RISERS)
        weight = hot(spot, count)
        out = []
        for axis in range(3):
            start = 2 * RISERS + axis * count
            speed = picked[start : start + count]
            value = -jnp.sum(jnp.where(weight, speed, 0.0), axis=0, keepdims=True)
            if axis < 2:
                some = picked[axis * RISERS : (axis + 1) * RISERS]
                value = value + jnp.sum(jnp.where(at_riser, some, 0.0), axis=0, keepdims=True)
            out.append(2.0 * value)
        return at_z, out

    contract = (((1,), (1,)), ((), ()))

    def parts(force):
        found = []
        for value in force:
            high, low = split(value)
            found.append((high.astype(f32), low.astype(f32)))
        return found

    def spread(count, spot, at_z, force):
        weight = hot(spot, count)
        halves = []
        for half in range(2):
            rows = [jnp.where(weight, value[half], 0.0) for value in parts(force)]
            halves.append(jnp.concatenate(rows, axis=0).astype(bf16))
        return lax.dot_general(
            jnp.concatenate(halves, axis=1),
            jnp.concatenate([at_z, at_z], axis=1),
            contract,
            preferred_element_type=f32,
        )

    def take(slab, attr, n):
        at = attr * 4 + 2 * n
        return jnp.concatenate([slab[at : at + 1, :], slab[at + 1 : at + 2, :]], axis=1)

    def halves_of(axis, column, count):
        value = smooth[axis, column * CELLS : (column + count) * CELLS, :]
        return jnp.concatenate(split(value), axis=1)

    sources = jnp.concatenate([goal, *(halves_of(axis, 0, CELLS) for axis in range(3))], axis=0)
    total = None
    for n in range(MARKS // step):
        here = slice(n * step, (n + 1) * step)
        mx, my, mz, riser = (
            m[:, here].astype(f32) for m in (own_x, own_y, own_z, own_riser)
        )
        spot = mx * CELLS + my
        _, force = force_of(sources, CELLS * CELLS, spot, mz, riser)
        where_z = hot(mz, DEPTH)
        halves = []
        for half in range(2):
            rows = [jnp.where(where_z, value[half], 0.0) for value in parts(force)]
            halves.append(jnp.concatenate(rows, axis=0).astype(bf16))
        at_cell = ones(hot(spot, CELLS * CELLS))
        got = lax.dot_general(
            jnp.concatenate([at_cell, at_cell], axis=1),
            jnp.concatenate(halves, axis=1),
            contract,
            preferred_element_type=f32,
        )
        total = got if total is None else total + got
        for axis in range(3):
            push[axis, :, here] = force[axis]
    for axis in range(3):
        impulse[axis, 1 : CELLS + 1] = total[:, axis * DEPTH : (axis + 1) * DEPTH].reshape(
            CELLS, CELLS, DEPTH
        )
    for message, at, spot_x in ((xlow, CELLS - 1, 0), (xhigh, 0, CELLS + 1)):
        column = (spot_x - 1) % FRAME
        sources = jnp.concatenate([goal, *(halves_of(axis, column, 1) for axis in range(3))], axis=0)
        slab = message[SLABS].astype(f32)
        total = None
        for n in range(MARKS // step):
            mx, my, mz, riser = (take(slab, attr, n) for attr in range(4))
            spot = jnp.where(mx == at, my, -1.0)
            at_z, force = force_of(sources, CELLS, spot, mz, riser)
            got = spread(CELLS, spot, at_z, force)
            total = got if total is None else total + got
        for axis in range(3):
            impulse[axis, spot_x] = total[axis * CELLS : (axis + 1) * CELLS]
    for s, (message, at) in enumerate(((ylow, CELLS - 1), (yhigh, 0))):
        halves = [jnp.concatenate(split(value), axis=1) for value in rim[s]]
        sources = jnp.concatenate([goal, *halves], axis=0)
        total = None
        for tile in range(3):
            slab = message[YSLABS + tile].astype(f32)
            for n in range(MARKS // step):
                mx, my, mz, riser = (take(slab, attr, n) for attr in range(4))
                keep = my == at
                if tile == 1:
                    keep = keep & (mx == CELLS - 1)
                elif tile == 2:
                    keep = keep & (mx == 0)
                spot = jnp.where(keep, mx + (0, 8, CELLS)[tile], -1.0)
                at_z, force = force_of(sources, FRAME, spot, mz, riser)
                got = spread(FRAME, spot, at_z, force)
                total = got if total is None else total + got
        for axis in range(3):
            lines[s, axis] = total[axis * FRAME : (axis + 1) * FRAME]

    @pl.loop(0, 18, unroll=3)
    def _(j):
        at = pl.ds(lax.rem(j + 23, FRAME), 1)
        for axis in range(3):
            value = impulse[axis, j]
            before = jnp.where(row == 0, lines[0, axis, at, :], spin(value, 1, 0))
            after = jnp.where(row == CELLS - 1, lines[1, axis, at, :], spin(value, -1, 0))
            tall[axis, j] = 0.5 * value + 0.25 * (before + after)

    def streamed(x, index):
        cx, cy, cz = VELOCITY[index]
        start = pl.multiple_of((x + (1 - cx)) * CELLS, CELLS)
        value = spin(spin(wide[index, pl.ds(start, CELLS), :], cy, 0), cz, 1)
        if cy:
            line = edge[0 if cy == 1 else 1, INWARD[cy].index(index), pl.ds(x, 1), :]
            value = jnp.where(row == (0 if cy == 1 else CELLS - 1), line, value)
        return (1.0 - rate) * value

    def collide(x):
        at = pl.ds(pl.multiple_of(x * CELLS, CELLS), CELLS)
        density = dens[0, at, :]
        own, speed = [], []
        for axis in range(3):
            value = 0.5 * tall[axis, x + 1] + 0.25 * (tall[axis, x] + tall[axis, x + 2])
            field[axis, x] = value
            own.append(value)
            speed.append((dens[1 + axis, at, :] + 0.5 * value) / density)
        square = speed[0] * speed[0] + speed[1] * speed[1] + speed[2] * speed[2]
        work = speed[0] * own[0] + speed[1] * own[1] + speed[2] * own[2]
        base = rate * density * (1.0 - 1.5 * square) - 3.0 * gain * work
        flow = [density * value for value in speed]
        even = [4.5 * rate * a + 9.0 * gain * b for a, b in zip(flow, own)]
        odd = [3.0 * rate * a + 3.0 * gain * b for a, b in zip(flow, own)]
        nxt[0, at, :] = streamed(x, 0) + WEIGHT[0] * base
        for weight, indices in ((WEIGHT[1], (1, 3, 5)), (WEIGHT[7], (7, 9, 11, 13, 15, 17))):
            scaled = weight * base
            wide_even = [weight * value for value in even]
            wide_odd = [weight * value for value in odd]
            for index in indices:
                direction = VELOCITY[index]
                both = scaled + along(speed, direction) * along(wide_even, direction)
                apart = along(wide_odd, direction)
                nxt[index, at, :] = streamed(x, index) + (both + apart)
                nxt[index + 1, at, :] = streamed(x, index + 1) + (both - apart)

    fetch.wait()
    copies = []
    chunk = 4
    for n in range(CELLS // chunk):

        @pl.loop(n * chunk, (n + 1) * chunk, unroll=2)
        def _(x):
            collide(x)

        cells_at = pl.ds(n * chunk * CELLS, chunk * CELLS)
        copies.append(
            pltpu.make_async_copy(nxt.at[:, cells_at, :], nxt_far.at[:, cells_at, :], sems.at[2 * n])
        )
        at = pl.ds(n * chunk, chunk)
        copies.append(pltpu.make_async_copy(field.at[:, at], field_far.at[:, at], sems.at[2 * n + 1]))
        for copy in copies[-2:]:
            copy.start()
    for copy in copies:
        copy.wait()


def on_device(populations, panels, modal_vel, marker_x, marker_y, marker_z, marker_riser):
    f32, bf16 = jnp.float32, jnp.bfloat16
    shape = jax.ShapeDtypeStruct
    devices = lax.axis_size("gx") * lax.axis_size("gy")
    cells = populations.reshape(19, CELLS * CELLS, DEPTH)
    marks = [m.reshape(1, MARKS) for m in (marker_x, marker_y, marker_z, marker_riser)]
    panel = panels.reshape(RISERS, -1)
    modes = panel.shape[1]
    vmem = pl.BlockSpec(memory_space=pltpu.VMEM)
    face = shape((SLABS + 1, CELLS, DEPTH), bf16)
    strip = shape((YSLABS + 3, FRAME, DEPTH), bf16)

    def limit(mib):
        return pltpu.CompilerParams(vmem_limit_bytes=mib << 20)

    anywhere = pl.BlockSpec(memory_space=pl.ANY)
    xup, xdown, rows = pl.pallas_call(
        pack_x,
        out_shape=(face, face, shape((devices, 128), f32)),
        in_specs=[anywhere] * 7,
        out_specs=(vmem,) * 3,
        scratch_shapes=[
            *[pltpu.VMEM((19, 3 * CELLS, DEPTH), f32)] * 2,
            *[pltpu.VMEM((1, MARKS), jnp.int32)] * 4,
            pltpu.VMEM(panel.shape, bf16),
            pltpu.VMEM(modal_vel.shape, bf16),
            pltpu.VMEM((16, DEPTH), f32),
            pltpu.VMEM((2 * RISERS, modes), f32),
            pltpu.SemaphoreType.DMA((8,)),
        ],
        name="pack_x",
    )(cells, *marks, panel, modal_vel)

    def ring(axis, toward):
        size = lax.axis_size(axis)
        return [(i, (i + toward) % size) for i in range(size)]

    xlow = lax.ppermute(xup, "gx", ring("gx", 1))
    xhigh = lax.ppermute(xdown, "gx", ring("gx", -1))
    table = lax.all_to_all(rows, ("gx", "gy"), 0, 0, tiled=True)
    yup, ydown = pl.pallas_call(
        pack_y,
        out_shape=(strip, strip),
        in_specs=[vmem] * 7,
        out_specs=(vmem,) * 2,
        scratch_shapes=[
            *[pltpu.VMEM((SLABS + 1, CELLS, DEPTH), f32)] * 2,
            pltpu.VMEM((16, DEPTH), f32),
        ],
        compiler_params=limit(8),
        name="pack_y",
    )(cells, xlow, xhigh, *marks)
    ylow = lax.ppermute(yup, "gy", ring("gy", 1))
    yhigh = lax.ppermute(ydown, "gy", ring("gy", -1))
    early = pl.pallas_call(
        columns,
        out_shape=shape((11, FRAME * CELLS, DEPTH), f32),
        in_specs=[vmem] * 3,
        out_specs=vmem,
        scratch_shapes=[
            pltpu.VMEM((19, 8 * CELLS, DEPTH), f32),
            pltpu.VMEM((3, 20, CELLS, DEPTH), f32),
        ],
        compiler_params=limit(12),
        name="columns",
    )(cells, xlow, xhigh)
    nxt, push, field = pl.pallas_call(
        step_kernel,
        out_shape=(
            shape((19, CELLS * CELLS, DEPTH), f32),
            shape((3, 1, MARKS), f32),
            shape((3, CELLS, CELLS, DEPTH), f32),
        ),
        in_specs=[anywhere] + [vmem] * 10,
        out_specs=(anywhere, vmem, anywhere),
        scratch_shapes=[
            pltpu.VMEM((19, (CELLS + 2) * CELLS, DEPTH), f32),
            pltpu.VMEM((19, CELLS * CELLS, DEPTH), f32),
            pltpu.VMEM((3, CELLS, CELLS, DEPTH), f32),
            pltpu.VMEM((2, INTO, FRAME, DEPTH), f32),
            pltpu.VMEM((2, 3, FRAME, DEPTH), f32),
            pltpu.VMEM((3, 18, CELLS, DEPTH), f32),
            pltpu.VMEM((3, FRAME * CELLS, DEPTH), f32),
            pltpu.VMEM((4, CELLS * CELLS, DEPTH), f32),
            pltpu.VMEM((3, 18, CELLS, DEPTH), f32),
            pltpu.SemaphoreType.DMA((9,)),
        ],
        compiler_params=limit(24),
        name="step_kernel",
    )(cells, early, xlow, xhigh, ylow, yhigh, *marks, table)
    return (
        nxt.reshape(19, CELLS, CELLS, DEPTH),
        push.transpose(1, 0, 2)[None],
        field,
    )


def solution(mesh):
    in_specs = (
        P(None, "gx", "gy", None),
        P(None, None, ("gx", "gy")),
        P(),
        P("gx", "gy", None),
        P("gx", "gy", None),
        P("gx", "gy", None),
        P("gx", "gy", None),
    )
    out_specs = (P(None, "gx", "gy", None), P("gx", "gy", None, None), P(None, "gx", "gy", None))
    return jax.shard_map(on_device, mesh=mesh, in_specs=in_specs, out_specs=out_specs, check_vma=False)
```

```python
import jax
import jax.numpy as jnp
from jax import lax
from jax.experimental import pallas as pl
from jax.experimental.pallas import tpu as pltpu
from jax.sharding import PartitionSpec as P

VELOCITY = (
    (0, 0, 0),
    (1, 0, 0),
    (-1, 0, 0),
    (0, 1, 0),
    (0, -1, 0),
    (0, 0, 1),
    (0, 0, -1),
    (1, 1, 0),
    (-1, -1, 0),
    (1, -1, 0),
    (-1, 1, 0),
    (1, 0, 1),
    (-1, 0, -1),
    (1, 0, -1),
    (-1, 0, 1),
    (0, 1, 1),
    (0, -1, -1),
    (0, 1, -1),
    (0, -1, 1),
)
WEIGHT = (1.0 / 3.0,) + (1.0 / 18.0,) * 6 + (1.0 / 36.0,) * 12
RELAX = 0.8
CELLS = 16
DEPTH = 128
MARKS = 512
RISERS = 64
FRAME = 24


def slabs(axis, toward):
    order = []
    for layer in (1, 2, 3):
        for index in range(19):
            if VELOCITY[index][axis] * toward >= layer - 2:
                order.append((layer, index))
    return order


ORDER = {(axis, toward): slabs(axis, toward) for axis in (0, 1) for toward in (1, -1)}
PLACE = {key: {slab: k for k, slab in enumerate(order)} for key, order in ORDER.items()}
SLABS = len(ORDER[0, 1])
INTO = 5
SUMS = 7
YSLABS = INTO + 2 * SUMS
STATE = 9
INWARD = {toward: [i for i in range(19) if VELOCITY[i][1] == toward] for toward in (1, -1)}


def near(layer, toward):
    return CELLS - layer if toward == 1 else layer - 1


def encode(value, index):
    return (value - WEIGHT[index]).astype(jnp.bfloat16)


def decode(value, index):
    return value.astype(jnp.float32) + WEIGHT[index]


def split(value):
    high = value.astype(jnp.bfloat16)
    low = (value - high.astype(jnp.float32)).astype(jnp.bfloat16)
    return high, low


def pack_x(
    cells_far, mx_far, my_far, mz_far, riser_far, panel_far, modal_far,
    xup, xdown, rows,
    first, last, mx, my, mz, riser, panel, modal, marks, pairs, sems,
):
    span = 3 * CELLS
    copies = [
        pltpu.make_async_copy(far, here, sems.at[n])
        for n, (far, here) in enumerate(
            (
                (modal_far, modal),
                (panel_far, panel),
                (mx_far, mx),
                (my_far, my),
                (mz_far, mz),
                (riser_far, riser),
                (cells_far.at[:, pl.ds(0, span), :], first),
                (cells_far.at[:, pl.ds(CELLS * CELLS - span, span), :], last),
            )
        )
    ]
    for copy in copies:
        copy.start()
    for copy in copies[:6]:
        copy.wait()
    fill_marks(marks, (mx, my, mz, riser))
    for n in range(RISERS):
        both = modal[n].astype(jnp.float32)
        for d in range(2):
            pairs[d * RISERS + n : d * RISERS + n + 1, :] = both[d : d + 1]
    product = lax.dot_general(
        panel[...],
        pairs[...].astype(jnp.bfloat16),
        (((1,), (1,)), ((), ())),
        preferred_element_type=jnp.float32,
    )
    mine = lax.broadcasted_iota(jnp.int32, product.shape, 0) == (
        lax.broadcasted_iota(jnp.int32, product.shape, 1) & (RISERS - 1)
    )
    row = jnp.sum(jnp.where(mine, product, 0.0), axis=0, keepdims=True)
    rows[...] = jnp.broadcast_to(row, rows.shape)
    for copy in copies[6:]:
        copy.wait()
    for out, toward in ((xup, 1), (xdown, -1)):
        for k, (layer, index) in enumerate(ORDER[0, toward]):
            if toward == 1:
                value = last[index, (3 - layer) * CELLS : (4 - layer) * CELLS, :]
            else:
                value = first[index, (layer - 1) * CELLS : layer * CELLS, :]
            out[k] = encode(value, index)
        out[SLABS] = marks[...].astype(jnp.bfloat16)


def fill_marks(marks, sources):
    for attr, source in enumerate(sources):
        for n in range(4):
            marks[attr * 4 + n : attr * 4 + n + 1, :] = source[:, n * 128 : (n + 1) * 128].astype(
                jnp.float32
            )


def pack_y(cells, xlow, xhigh, mx, my, mz, riser, yup, ydown, low, high, marks):
    low[...] = xlow[...].astype(jnp.float32)
    high[...] = xhigh[...].astype(jnp.float32)
    fill_marks(marks, (mx, my, mz, riser))
    place = lax.broadcasted_iota(jnp.int32, (8, DEPTH), 0)
    none = jnp.zeros((8, DEPTH), jnp.float32)

    def frame(layer, index, toward):
        row = near(layer, toward)
        tile = none
        for depth in (1, 2, 3):
            for source, side, at in ((high, -1, depth - 1), (low, 1, 8 - depth)):
                slot = PLACE[0, side].get((depth, index))
                if slot is not None:
                    tile = jnp.where(place == at, source[slot, row : row + 1, :], tile)
        own = cells[index, pl.ds(row, CELLS, stride=CELLS), :] - WEIGHT[index]
        return jnp.concatenate([own, tile], axis=0)

    for out, toward in ((yup, 1), (ydown, -1)):
        for n, index in enumerate(INWARD[toward]):
            out[n] = frame(1, index, toward).astype(jnp.bfloat16)

        def reads(cell):
            for index in range(19):
                cx, cy, cz = VELOCITY[index]
                layer = cell + toward * cy
                if layer:
                    value = frame(layer, index, toward) + WEIGHT[index]
                    yield index, spin(spin(value, cx, 0), cz, 1)

        density, momentum = moments(reads(2))
        sums = [value / density for value in momentum]
        density, momentum = moments(reads(1))
        for k, value in enumerate([*sums, density, *momentum]):
            out[INTO + 2 * k], out[INTO + 2 * k + 1] = split(value)
        for n, source in enumerate((marks[...], low[SLABS], high[SLABS])):
            out[YSLABS + n] = jnp.concatenate([source, none], axis=0).astype(jnp.bfloat16)


def moments(reads):
    density = None
    momentum = [None, None, None]
    for index, value in reads:
        density = value if density is None else density + value
        for axis in range(3):
            sign = VELOCITY[index][axis]
            if sign == 1:
                momentum[axis] = value if momentum[axis] is None else momentum[axis] + value
            elif sign == -1:
                momentum[axis] = -value if momentum[axis] is None else momentum[axis] - value
    return density, momentum


def along(vector, direction):
    total = None
    for axis in range(3):
        if direction[axis] == 1:
            total = vector[axis] if total is None else total + vector[axis]
        elif direction[axis] == -1:
            total = -vector[axis] if total is None else total - vector[axis]
    return total


def spin(value, shift, axis):
    return pltpu.roll(value, shift % value.shape[axis], axis) if shift else value


def views(state):
    return state.at[pl.ds(0, 4)], state.at[pl.ds(4, 3)]


def spare(n):
    return 7 + n // 16, slice((n % 16) * FRAME, (n % 16 + 1) * FRAME)


def inner_spot(side, row, axis):
    return spare(8 + 6 * side + 3 * (row - 1) + axis)


def columns(cells, xlow, xhigh, state_far, state, vel, side, tall, sem):
    sums, smooth = views(state)

    def rows_of(column):
        return slice(column * CELLS, (column + 1) * CELLS)

    for message, toward in ((xlow, 1), (xhigh, -1)):
        for k, (layer, index) in enumerate(ORDER[0, toward]):
            column = 8 - layer if toward == 1 else layer - 1
            side[index, rows_of(column), :] = decode(message[k], index)

    for s, toward in enumerate((1, -1)):
        first = 0 if toward == 1 else CELLS - 1

        def outward():
            for index in INWARD[-toward]:
                cx, _, cz = VELOCITY[index]
                value = jnp.concatenate(
                    [
                        cells[index, pl.ds(first, CELLS, stride=CELLS), :],
                        side[index, pl.ds(first, 8, stride=CELLS), :],
                    ],
                    axis=0,
                )
                yield index, spin(spin(value, cx, 0), cz, 1)

        density, momentum = moments(outward())
        for k, value in enumerate([density, *momentum]):
            plane, here = spare(4 * s + k)
            state[plane, here, :] = value

    row = lax.broadcasted_iota(jnp.int32, (CELLS, DEPTH), 0)

    def one(x, known):
        if known:
            here = rows_of(x % FRAME)
        else:
            here = pl.ds(pl.multiple_of(x * CELLS, CELLS), CELLS)

        def reads():
            for index in range(19):
                cx, cy, cz = VELOCITY[index]
                if known:
                    at = (x - cx) % FRAME
                    if at < CELLS:
                        value = cells[index, rows_of(at), :]
                    else:
                        value = side[index, rows_of(at - CELLS), :]
                else:
                    at = x - cx
                    value = cells[index, pl.ds(pl.multiple_of(at * CELLS, CELLS), CELLS), :]
                if cy:
                    value = jnp.where(row == (0 if cy == 1 else CELLS - 1), 0.0, spin(value, cy, 0))
                value = spin(value, cz, 1)
                yield index, value

        density, momentum = moments(reads())
        sums[0, here, :] = density
        for axis in range(3):
            sums[1 + axis, here, :] = momentum[axis]
            vel[axis, here, :] = momentum[axis] / density

    for x in (-2, -1, 0, CELLS - 1, CELLS, CELLS + 1):
        one(x, True)

    @pl.loop(1, CELLS - 1)
    def _(x):
        one(x, False)

    def start(x):
        return pl.ds(pl.multiple_of(lax.rem(x + FRAME, FRAME) * CELLS, CELLS), CELLS)

    @pl.loop(0, 20, unroll=4)
    def _(j):
        for axis in range(3):
            value = vel[axis, start(j - 2), :]
            tall[axis, j] = 0.5 * value + 0.25 * (spin(value, 1, 0) + spin(value, -1, 0))

    @pl.loop(0, 18, unroll=3)
    def _(j):
        for axis in range(3):
            smooth[axis, start(j - 1), :] = 0.5 * tall[axis, j + 1] + 0.25 * (
                tall[axis, j] + tall[axis, j + 2]
            )

    for s, toward in enumerate((1, -1)):
        first = 0 if toward == 1 else CELLS - 1
        for inner_row in (1, 2):
            for axis in range(3):
                plane, here = inner_spot(s, inner_row, axis)
                spots = pl.ds(first + inner_row * toward, FRAME, stride=CELLS)
                state[plane, here, :] = vel[axis, spots, :]
    keeping = pltpu.make_async_copy(state, state_far.at[pl.ds(0, STATE)], sem)
    keeping.start()
    keeping.wait()


def step_kernel(
    cells_far, state_far, xlow, xhigh, ylow, yhigh, own_x, own_y, own_z, own_riser, table,
    nxt_far, push, field_far,
    wide, nxt, field, edge, lines, tall, smooth, dens, share, impulse, sems,
):
    f32, bf16 = jnp.float32, jnp.bfloat16
    rate = 1.0 / RELAX
    gain = 1.0 - 0.5 / RELAX
    row = lax.broadcasted_iota(jnp.int32, (CELLS, DEPTH), 0)
    place = lax.broadcasted_iota(jnp.int32, (FRAME, DEPTH), 0)
    inside = (place <= CELLS) | (place == FRAME - 1)
    sums = dens
    early = []
    for n, (first, here) in enumerate(((0, dens), (4, smooth), (7, share))):
        planes = state_far.at[pl.ds(first, here.shape[0])]
        early.append(pltpu.make_async_copy(planes, here, sems.at[9 + n]))
    for copy in early:
        copy.start()
    fetch = pltpu.make_async_copy(
        cells_far, wide.at[:, pl.ds(CELLS, CELLS * CELLS), :], sems.at[8]
    )
    fetch.start()
    for message, toward in ((xlow, 1), (xhigh, -1)):
        column = 0 if toward == 1 else CELLS + 1
        for index in range(19):
            if VELOCITY[index][0] == toward:
                here = slice(column * CELLS, (column + 1) * CELLS)
                wide[index, here, :] = decode(message[PLACE[0, toward][1, index]], index)
    goal = jnp.concatenate(split(table[...].T), axis=1)
    for copy in early:
        copy.wait()

    def over_x(value):
        return 0.5 * value + 0.25 * (spin(value, 1, 0) + spin(value, -1, 0))

    rim = [[], []]
    for s, (toward, message) in enumerate(((1, ylow), (-1, yhigh))):
        first = 0 if toward == 1 else CELLS - 1

        def crossing():
            for n, index in enumerate(INWARD[toward]):
                cx, _, cz = VELOCITY[index]
                value = spin(spin(decode(message[n], index), cx, 0), cz, 1)
                edge[s, n] = value
                yield index, value

        density, momentum = moments(crossing())
        whole = []
        for k, value in enumerate([density, *momentum]):
            value = value + sums[k, pl.ds(first, FRAME, stride=CELLS), :]
            dens[k, pl.ds(first, CELLS, stride=CELLS), :] = value[:CELLS]
            whole.append(value)
        sent = [
            message[INTO + 2 * k].astype(f32) + message[INTO + 2 * k + 1].astype(f32)
            for k in range(SUMS)
        ]
        outer = []
        for k in range(4):
            plane, here = spare(4 * s + k)
            outer.append(sent[3 + k] + share[plane - 7, here, :])
        for axis in range(3):
            beyond = outer[1 + axis] / outer[0]
            at_edge = whole[1 + axis] / whole[0]
            second = pl.ds(first + toward, FRAME, stride=CELLS)
            plane, here = inner_spot(s, 1, axis)
            inner = share[plane - 7, here, :]
            plane, here = inner_spot(s, 2, axis)
            third = share[plane - 7, here, :]
            smooth[axis, pl.ds(first, FRAME, stride=CELLS), :] = over_x(
                0.5 * at_edge + 0.25 * (beyond + inner)
            )
            smooth[axis, second, :] = over_x(0.5 * inner + 0.25 * (at_edge + third))
            value = over_x(0.5 * beyond + 0.25 * (sent[axis] + at_edge))
            rim[s].append(jnp.where(inside, value, 0.0))

    step = 256

    def hot(position, count):
        shape = (count, position.shape[1])
        return lax.broadcasted_iota(jnp.int32, shape, 0).astype(f32) == position

    def ones(mask):
        return jnp.where(mask, 1.0, 0.0).astype(bf16)

    def force_of(sources, count, spot, z, riser):
        at_z = ones(hot(z, DEPTH))
        picked = jnp.dot(
            sources, jnp.concatenate([at_z, at_z], axis=0), preferred_element_type=f32
        )
        at_riser = hot(riser, RISERS)
        weight = hot(spot, count)
        out = []
        for axis in range(3):
            start = 2 * RISERS + axis * count
            speed = picked[start : start + count]
            value = -jnp.sum(jnp.where(weight, speed, 0.0), axis=0, keepdims=True)
            if axis < 2:
                some = picked[axis * RISERS : (axis + 1) * RISERS]
                value = value + jnp.sum(jnp.where(at_riser, some, 0.0), axis=0, keepdims=True)
            out.append(2.0 * value)
        return at_z, out

    contract = (((1,), (1,)), ((), ()))

    def parts(force):
        found = []
        for value in force:
            high, low = split(value)
            found.append((high.astype(f32), low.astype(f32)))
        return found

    def spread(count, spot, at_z, force):
        weight = hot(spot, count)
        halves = []
        for half in range(2):
            rows = [jnp.where(weight, value[half], 0.0) for value in parts(force)]
            halves.append(jnp.concatenate(rows, axis=0).astype(bf16))
        return lax.dot_general(
            jnp.concatenate(halves, axis=1),
            jnp.concatenate([at_z, at_z], axis=1),
            contract,
            preferred_element_type=f32,
        )

    def take(slab, attr, n):
        at = attr * 4 + 2 * n
        return jnp.concatenate([slab[at : at + 1, :], slab[at + 1 : at + 2, :]], axis=1)

    def halves_of(axis, column, count):
        value = smooth[axis, column * CELLS : (column + count) * CELLS, :]
        return jnp.concatenate(split(value), axis=1)

    sources = jnp.concatenate([goal, *(halves_of(axis, 0, CELLS) for axis in range(3))], axis=0)
    total = None
    for n in range(MARKS // step):
        here = slice(n * step, (n + 1) * step)
        mx, my, mz, riser = (
            m[:, here].astype(f32) for m in (own_x, own_y, own_z, own_riser)
        )
        spot = mx * CELLS + my
        _, force = force_of(sources, CELLS * CELLS, spot, mz, riser)
        where_z = hot(mz, DEPTH)
        halves = []
        for half in range(2):
            rows = [jnp.where(where_z, value[half], 0.0) for value in parts(force)]
            halves.append(jnp.concatenate(rows, axis=0).astype(bf16))
        at_cell = ones(hot(spot, CELLS * CELLS))
        got = lax.dot_general(
            jnp.concatenate([at_cell, at_cell], axis=1),
            jnp.concatenate(halves, axis=1),
            contract,
            preferred_element_type=f32,
        )
        total = got if total is None else total + got
        for axis in range(3):
            push[axis, :, here] = force[axis]
    for axis in range(3):
        impulse[axis, 1 : CELLS + 1] = total[:, axis * DEPTH : (axis + 1) * DEPTH].reshape(
            CELLS, CELLS, DEPTH
        )
    for message, at, spot_x in ((xlow, CELLS - 1, 0), (xhigh, 0, CELLS + 1)):
        column = (spot_x - 1) % FRAME
        sources = jnp.concatenate([goal, *(halves_of(axis, column, 1) for axis in range(3))], axis=0)
        slab = message[SLABS].astype(f32)
        total = None
        for n in range(MARKS // step):
            mx, my, mz, riser = (take(slab, attr, n) for attr in range(4))
            spot = jnp.where(mx == at, my, -1.0)
            at_z, force = force_of(sources, CELLS, spot, mz, riser)
            got = spread(CELLS, spot, at_z, force)
            total = got if total is None else total + got
        for axis in range(3):
            impulse[axis, spot_x] = total[axis * CELLS : (axis + 1) * CELLS]
    for s, (message, at) in enumerate(((ylow, CELLS - 1), (yhigh, 0))):
        halves = [jnp.concatenate(split(value), axis=1) for value in rim[s]]
        sources = jnp.concatenate([goal, *halves], axis=0)
        total = None
        for tile in range(3):
            slab = message[YSLABS + tile].astype(f32)
            for n in range(MARKS // step):
                mx, my, mz, riser = (take(slab, attr, n) for attr in range(4))
                keep = my == at
                if tile == 1:
                    keep = keep & (mx == CELLS - 1)
                elif tile == 2:
                    keep = keep & (mx == 0)
                spot = jnp.where(keep, mx + (0, 8, CELLS)[tile], -1.0)
                at_z, force = force_of(sources, FRAME, spot, mz, riser)
                got = spread(FRAME, spot, at_z, force)
                total = got if total is None else total + got
        for axis in range(3):
            lines[s, axis] = total[axis * FRAME : (axis + 1) * FRAME]

    @pl.loop(0, 18, unroll=3)
    def _(j):
        at = pl.ds(lax.rem(j + 23, FRAME), 1)
        for axis in range(3):
            value = impulse[axis, j]
            before = jnp.where(row == 0, lines[0, axis, at, :], spin(value, 1, 0))
            after = jnp.where(row == CELLS - 1, lines[1, axis, at, :], spin(value, -1, 0))
            tall[axis, j] = 0.5 * value + 0.25 * (before + after)

    def streamed(x, index):
        cx, cy, cz = VELOCITY[index]
        start = pl.multiple_of((x + (1 - cx)) * CELLS, CELLS)
        value = spin(spin(wide[index, pl.ds(start, CELLS), :], cy, 0), cz, 1)
        if cy:
            line = edge[0 if cy == 1 else 1, INWARD[cy].index(index), pl.ds(x, 1), :]
            value = jnp.where(row == (0 if cy == 1 else CELLS - 1), line, value)
        return (1.0 - rate) * value

    def collide(x):
        at = pl.ds(pl.multiple_of(x * CELLS, CELLS), CELLS)
        density = dens[0, at, :]
        own, speed = [], []
        for axis in range(3):
            value = 0.5 * tall[axis, x + 1] + 0.25 * (tall[axis, x] + tall[axis, x + 2])
            field[axis, x] = value
            own.append(value)
            speed.append((dens[1 + axis, at, :] + 0.5 * value) / density)
        square = speed[0] * speed[0] + speed[1] * speed[1] + speed[2] * speed[2]
        work = speed[0] * own[0] + speed[1] * own[1] + speed[2] * own[2]
        base = rate * density * (1.0 - 1.5 * square) - 3.0 * gain * work
        flow = [density * value for value in speed]
        even = [4.5 * rate * a + 9.0 * gain * b for a, b in zip(flow, own)]
        odd = [3.0 * rate * a + 3.0 * gain * b for a, b in zip(flow, own)]
        nxt[0, at, :] = streamed(x, 0) + WEIGHT[0] * base
        for weight, indices in ((WEIGHT[1], (1, 3, 5)), (WEIGHT[7], (7, 9, 11, 13, 15, 17))):
            scaled = weight * base
            wide_even = [weight * value for value in even]
            wide_odd = [weight * value for value in odd]
            for index in indices:
                direction = VELOCITY[index]
                both = scaled + along(speed, direction) * along(wide_even, direction)
                apart = along(wide_odd, direction)
                nxt[index, at, :] = streamed(x, index) + (both + apart)
                nxt[index + 1, at, :] = streamed(x, index + 1) + (both - apart)

    fetch.wait()
    copies = []
    chunk = 4
    for n in range(CELLS // chunk):

        @pl.loop(n * chunk, (n + 1) * chunk, unroll=4)
        def _(x):
            collide(x)

        cells_at = pl.ds(n * chunk * CELLS, chunk * CELLS)
        copies.append(
            pltpu.make_async_copy(nxt.at[:, cells_at, :], nxt_far.at[:, cells_at, :], sems.at[2 * n])
        )
        at = pl.ds(n * chunk, chunk)
        copies.append(pltpu.make_async_copy(field.at[:, at], field_far.at[:, at], sems.at[2 * n + 1]))
        for copy in copies[-2:]:
            copy.start()
    for copy in copies:
        copy.wait()


def on_device(populations, panels, modal_vel, marker_x, marker_y, marker_z, marker_riser):
    f32, bf16 = jnp.float32, jnp.bfloat16
    shape = jax.ShapeDtypeStruct
    devices = lax.axis_size("gx") * lax.axis_size("gy")
    cells = populations.reshape(19, CELLS * CELLS, DEPTH)
    marks = [m.reshape(1, MARKS) for m in (marker_x, marker_y, marker_z, marker_riser)]
    panel = panels.reshape(RISERS, -1)
    modes = panel.shape[1]
    vmem = pl.BlockSpec(memory_space=pltpu.VMEM)
    face = shape((SLABS + 1, CELLS, DEPTH), bf16)
    strip = shape((YSLABS + 3, FRAME, DEPTH), bf16)

    def limit(mib):
        return pltpu.CompilerParams(vmem_limit_bytes=mib << 20)

    anywhere = pl.BlockSpec(memory_space=pl.ANY)
    xup, xdown, rows = pl.pallas_call(
        pack_x,
        out_shape=(face, face, shape((devices, 128), f32)),
        in_specs=[anywhere] * 7,
        out_specs=(vmem,) * 3,
        scratch_shapes=[
            *[pltpu.VMEM((19, 3 * CELLS, DEPTH), f32)] * 2,
            *[pltpu.VMEM((1, MARKS), jnp.int32)] * 4,
            pltpu.VMEM(panel.shape, bf16),
            pltpu.VMEM(modal_vel.shape, bf16),
            pltpu.VMEM((16, DEPTH), f32),
            pltpu.VMEM((2 * RISERS, modes), f32),
            pltpu.SemaphoreType.DMA((8,)),
        ],
        name="pack_x",
    )(cells, *marks, panel, modal_vel)

    def ring(axis, toward):
        size = lax.axis_size(axis)
        return [(i, (i + toward) % size) for i in range(size)]

    xlow = lax.ppermute(xup, "gx", ring("gx", 1))
    xhigh = lax.ppermute(xdown, "gx", ring("gx", -1))
    table = lax.all_to_all(rows, ("gx", "gy"), 0, 0, tiled=True)
    yup, ydown = pl.pallas_call(
        pack_y,
        out_shape=(strip, strip),
        in_specs=[vmem] * 7,
        out_specs=(vmem,) * 2,
        scratch_shapes=[
            *[pltpu.VMEM((SLABS + 1, CELLS, DEPTH), f32)] * 2,
            pltpu.VMEM((16, DEPTH), f32),
        ],
        compiler_params=limit(8),
        name="pack_y",
    )(cells, xlow, xhigh, *marks)
    ylow = lax.ppermute(yup, "gy", ring("gy", 1))
    yhigh = lax.ppermute(ydown, "gy", ring("gy", -1))
    early = pl.pallas_call(
        columns,
        out_shape=shape((12 * STATE, FRAME * CELLS, DEPTH), f32),
        in_specs=[vmem] * 3,
        out_specs=anywhere,
        scratch_shapes=[
            pltpu.VMEM((STATE, FRAME * CELLS, DEPTH), f32),
            pltpu.VMEM((3, FRAME * CELLS, DEPTH), f32),
            pltpu.VMEM((19, 8 * CELLS, DEPTH), f32),
            pltpu.VMEM((3, 20, CELLS, DEPTH), f32),
            pltpu.SemaphoreType.DMA,
        ],
        compiler_params=limit(48),
        name="columns",
    )(cells, xlow, xhigh)
    nxt, push, field = pl.pallas_call(
        step_kernel,
        out_shape=(
            shape((19, CELLS * CELLS, DEPTH), f32),
            shape((3, 1, MARKS), f32),
            shape((3, CELLS, CELLS, DEPTH), f32),
        ),
        in_specs=[anywhere] * 2 + [vmem] * 9,
        out_specs=(anywhere, vmem, anywhere),
        scratch_shapes=[
            pltpu.VMEM((19, (CELLS + 2) * CELLS, DEPTH), f32),
            pltpu.VMEM((19, CELLS * CELLS, DEPTH), f32),
            pltpu.VMEM((3, CELLS, CELLS, DEPTH), f32),
            pltpu.VMEM((2, INTO, FRAME, DEPTH), f32),
            pltpu.VMEM((2, 3, FRAME, DEPTH), f32),
            pltpu.VMEM((3, 18, CELLS, DEPTH), f32),
            pltpu.VMEM((3, FRAME * CELLS, DEPTH), f32),
            pltpu.VMEM((4, FRAME * CELLS, DEPTH), f32),
            pltpu.VMEM((2, FRAME * CELLS, DEPTH), f32),
            pltpu.VMEM((3, 18, CELLS, DEPTH), f32),
            pltpu.SemaphoreType.DMA((13,)),
        ],
        compiler_params=limit(48),
        name="step_kernel",
    )(cells, early, xlow, xhigh, ylow, yhigh, *marks, table)
    return (
        nxt.reshape(19, CELLS, CELLS, DEPTH),
        push.transpose(1, 0, 2)[None],
        field,
    )


def solution(mesh):
    in_specs = (
        P(None, "gx", "gy", None),
        P(None, None, ("gx", "gy")),
        P(),
        P("gx", "gy", None),
        P("gx", "gy", None),
        P("gx", "gy", None),
        P("gx", "gy", None),
    )
    out_specs = (P(None, "gx", "gy", None), P("gx", "gy", None, None), P(None, "gx", "gy", None))
    return jax.shard_map(on_device, mesh=mesh, in_specs=in_specs, out_specs=out_specs, check_vma=False)
```
